256 devices in a mesh: seq: 32 (over y, z), tp: 8 (over x, core).
Axes of the slice: x: 4, y: 4, z: 8, core: 2. Of those that a mesh axis runs over, the one named last changes fastest.
Arguments:
- queries: bfloat16 [16384, 4096], P('seq', 'tp'), may hold values from -36 to 36
- new_keys: bfloat16 [16384, 1024], P('seq', 'tp'), may hold values from -9 to 9
- new_values: bfloat16 [16384, 1024], P('seq', 'tp'), may hold values from -6 to 6
- key_cache: bfloat16 [131072, 1024], P('seq', 'tp'), may hold values from -6 to 6
- value_cache: bfloat16 [131072, 1024], P('seq', 'tp'), may hold values from -6 to 6
- block_lists: int32 [128, 8], P('seq'), may hold values from 0 to 1023, as said below
- out_weight: bfloat16 [4096, 8192], P('tp'), may hold values from -0.09375 to 0.09375
Outputs:
- output: bfloat16 [16384, 8192], P('seq', 'tp')
The draws below stay inside these ranges and needn't reach their ends.
Inputs may be any that keep to these rules, and one draw needn't show every extreme that they name: For each index of seq, the 32 entries of its rows of block_lists lie at most 4 in the blocks of any one index of seq (blocks s * 32 to (s + 1) * 32 - 1), and some such range holds exactly 4 of them; the entries of one row differ.
All inputs are finite; a program needn't handle non-finite values.
Results may differ from the reference program's by a relative error of at most 0.017.
Values may be sent and summed in bfloat16 or wider, within the bound.
A program may use at most 128 MiB of HBM per device.

```python
import math
import jax
import jax.numpy as jnp
from jax import lax

D = 8192
KVH = 8
HD = 128
QH = 32
BLOCK = 128
TOPB = 8
SPAN = 16384
CTX = 131072
QBD = 4
QB = 128
BLK_DEV = 32
CTX_BLOCKS = 1024
FETCH = 4
N_TP = 8


def draw_queries(key, part):
    drawn = jnp.clip(jax.random.normal(jax.random.fold_in(key, 1), (SPAN, QH * HD), jnp.float32), -6.0, 6.0)
    return drawn.astype(jnp.bfloat16)


def draw_new_keys(key, part):
    drawn = jnp.clip(jax.random.normal(jax.random.fold_in(key, 3), (SPAN, KVH * HD), jnp.float32), -6.0, 6.0)
    return drawn.astype(jnp.bfloat16)


def draw_block_lists(key, part):
    devices = QB // QBD
    slot_count = QBD * TOPB
    shard_count = CTX_BLOCKS // BLK_DEV
    slot_limit = shard_count * FETCH
    random_integers = jax.random.randint(jax.random.fold_in(key, 11), (devices, slot_limit), 0, 4096)
    shard_heat = jax.random.randint(jax.random.fold_in(key, 12), (shard_count,), 0, 3) * 2048
    slot_heat_levels = jnp.repeat(shard_heat, FETCH)
    preferred_slots = jax.random.randint(jax.random.fold_in(key, 13), (devices, 1), 0, shard_count)
    slot_owner_shard = jnp.arange(slot_limit, dtype=jnp.int32) // FETCH
    extra_credit = jnp.where(slot_owner_shard[None, :] == preferred_slots, 16384, 0)
    slot_ranking = (random_integers + slot_heat_levels[None, :] + extra_credit) * slot_limit + jnp.arange(slot_limit, dtype=jnp.int32)[None, :]
    unused, picked = lax.top_k(slot_ranking, slot_count)
    shuffle_keys = jax.random.randint(jax.random.fold_in(key, 14), (devices, slot_count), 0, 1 << 20) * slot_count + jnp.arange(slot_count, dtype=jnp.int32)[None, :]
    shuffle = jnp.argsort(shuffle_keys, axis=1)
    picked = jnp.take_along_axis(picked, shuffle, axis=1)
    shard_of = picked // FETCH
    turn_of = picked % FETCH
    start_local = jax.random.randint(jax.random.fold_in(key, 15), (devices, shard_count), 0, BLK_DEV)
    stride_local = jax.random.randint(jax.random.fold_in(key, 16), (devices, shard_count), 1, BLK_DEV // FETCH + 1)
    local_block = (jnp.take_along_axis(start_local, shard_of, axis=1) + turn_of * jnp.take_along_axis(stride_local, shard_of, axis=1)) % BLK_DEV
    return (shard_of * BLK_DEV + local_block).reshape(QB, TOPB).astype(jnp.int32)


def shard_levels(own_key, extent, split, low, high):
    loudness, own = 1.0, jax.random.fold_in(own_key, 6)
    for axis_at, blocks in split:
        steps = jnp.exp(jax.random.uniform(jax.random.fold_in(own, axis_at), (blocks,), jnp.float32, low / len(split), high / len(split)))
        loudness = loudness * jnp.repeat(steps, extent[axis_at] // blocks).reshape([-1 if axis == axis_at else 1 for axis in range(len(extent))])
    return loudness


def centred(own_key, dims, width, reach, cuts=(), kind=jnp.bfloat16):
    drawn = width * jax.random.normal(own_key, dims, jnp.float32)
    if cuts:
        drawn = drawn * shard_levels(own_key, dims, cuts, -0.22, 0.18)
    return jnp.clip(drawn, -reach, reach).astype(kind)


def setup_inputs(seed: int = 0) -> dict:
    splits = jax.random.split(jax.random.key(seed), 8)
    return {
        "queries": draw_queries(jax.random.fold_in(splits[7], 71), 0),
        "new_keys": draw_new_keys(jax.random.fold_in(splits[7], 71), 0),
        "new_values": centred(splits[2], (SPAN, KVH * HD), 1.0, 6.0, ((0, 32), (1, 8))),
        "key_cache": centred(splits[3], (CTX, KVH * HD), 1.0, 6.0, ((0, 32), (1, 8))),
        "value_cache": centred(splits[4], (CTX, KVH * HD), 1.0, 6.0, ((0, 32), (1, 8))),
        "block_lists": draw_block_lists(jax.random.fold_in(splits[7], 71), 0),
        "out_weight": centred(splits[6], (QH * HD, D), (QH * HD) ** -0.5, 0.09375, ((0, 8),)),
    }


def reference(queries, new_keys, new_values, key_cache, value_cache, block_lists, out_weight):
    heads_per_kv = QH // KVH
    query_blocks = SPAN // BLOCK
    score_scale = 1.0 / math.sqrt(HD)
    cache_keys = key_cache.reshape(CTX // BLOCK, BLOCK, KVH, HD)
    cache_values = value_cache.reshape(CTX // BLOCK, BLOCK, KVH, HD)
    query_tiles = queries.reshape(query_blocks, BLOCK, KVH, heads_per_kv, HD)
    fresh_keys = new_keys.reshape(query_blocks, BLOCK, KVH, HD)
    fresh_values = new_values.reshape(query_blocks, BLOCK, KVH, HD)
    listed_rows = TOPB * BLOCK
    row_ids = jnp.arange(BLOCK, dtype=jnp.int32)[:, None]
    col_ids = jnp.arange(listed_rows + BLOCK, dtype=jnp.int32)[None, :]
    visible = (col_ids < listed_rows) | (col_ids - listed_rows <= row_ids)

    def attend(pieces):
        query_tile, chosen, own_keys, own_values = pieces
        all_keys = jnp.concatenate([cache_keys[chosen].reshape(listed_rows, KVH, HD), own_keys], axis=0)
        all_values = jnp.concatenate([cache_values[chosen].reshape(listed_rows, KVH, HD), own_values], axis=0)
        scores = jnp.einsum('ikgd,jkd->kgij', query_tile.astype(jnp.float32), all_keys.astype(jnp.float32)) * score_scale
        scores = jnp.where(visible[None, None], scores, -1e+30)
        largest = lax.optimization_barrier(jnp.max(scores, axis=-1, keepdims=True))
        expanded = jnp.exp(scores - largest)
        weights = (expanded / lax.optimization_barrier(jnp.sum(expanded, axis=-1, keepdims=True))).astype(jnp.bfloat16)
        mixed = jnp.einsum('kgij,jkd->ikgd', weights.astype(jnp.float32), all_values.astype(jnp.float32))
        return mixed.astype(jnp.bfloat16).reshape(BLOCK, QH * HD)
    attended = lax.map(attend, (query_tiles, block_lists, fresh_keys, fresh_values)).reshape(SPAN, QH * HD)
    group_rows = QH * HD // N_TP
    summed = jnp.zeros((SPAN, D), jnp.float32)
    for tp_group in range(N_TP):
        start_row = tp_group * group_rows
        partial_value = jnp.dot(attended[:, start_row:start_row + group_rows], out_weight[start_row:start_row + group_rows], preferred_element_type=jnp.float32).astype(jnp.bfloat16)
        partial_value = lax.optimization_barrier(partial_value)
        summed = summed + partial_value.astype(jnp.float32)
    return summed.astype(jnp.bfloat16)
```

```python
import functools
import math

import jax
import jax.numpy as jnp
from jax import lax
from jax.experimental import pallas as pl
from jax.experimental.pallas import tpu as pltpu
from jax.sharding import PartitionSpec as P

HD = 128
BLOCK = 128
TOPB = 8
NY, NZ, NX, NC = 4, 8, 4, 2
SEQ = NY * NZ
TP = NX * NC
SHARD = 32
QBD = 4
ENT = QBD * TOPB
G = 4
CAPS = (8, 24, 32, 32)
PARTS = 2
ROWS = BLOCK // PARTS
CHUNKS = 2 * PARTS
MESH = pl.DeviceIdType.MESH
F32 = jnp.float32
BF16 = jnp.bfloat16


def lists_kernel(own_ref, out_ref, send_sem, recv_sem):
    me = lax.axis_index("seq")
    barrier = pltpu.get_barrier_semaphore()

    def greet(i, carry):
        peer = lax.rem(me + i, SEQ)
        pl.semaphore_signal(barrier, inc=1, device_id={"seq": peer}, device_id_type=MESH)
        return carry

    lax.fori_loop(1, SEQ, greet, 0)
    pl.semaphore_wait(barrier, SEQ - 1)

    def copy(i):
        peer = lax.rem(me + i, SEQ)
        return pltpu.make_async_remote_copy(
            src_ref=own_ref,
            dst_ref=out_ref.at[me],
            send_sem=send_sem.at[i],
            recv_sem=recv_sem.at[i],
            device_id={"seq": peer},
            device_id_type=MESH,
        )

    def start(i, carry):
        copy(i).start()
        return carry

    lax.fori_loop(1, SEQ, start, 0)
    out_ref[me] = own_ref[...]

    def finish(i, carry):
        copy(i).wait()
        return carry

    lax.fori_loop(1, SEQ, finish, 0)


def gather_lists(block_lists):
    padded = jnp.pad(block_lists.reshape(1, ENT), ((0, 7), (0, 128 - ENT)))
    every = pl.pallas_call(
        lists_kernel,
        out_shape=jax.ShapeDtypeStruct((SEQ, 8, 128), jnp.int32),
        in_specs=[pl.BlockSpec(memory_space=pltpu.VMEM)],
        out_specs=pl.BlockSpec(memory_space=pltpu.VMEM),
        scratch_shapes=[
            pltpu.SemaphoreType.DMA((SEQ,)),
            pltpu.SemaphoreType.DMA((SEQ,)),
        ],
        compiler_params=pltpu.CompilerParams(collective_id=0, has_side_effects=True),
        name="gather_lists",
    )(padded)
    return every[:, 0, :ENT]


def route_tables(every):
    me = lax.axis_index("seq")
    y, z = me // NZ, me % NZ
    row = lax.dynamic_slice_in_dim(every, y * NZ, NZ, axis=0)
    rel = lax.dynamic_slice_in_dim(jnp.concatenate([row, row], axis=0), z, NZ, axis=0)
    k = jnp.arange(NZ, dtype=jnp.int32)[:, None]
    owner = rel // SHARD
    spot = (owner // NZ) * SHARD + rel % SHARD
    du = (z + k - owner % NZ + NZ) % NZ
    e = jnp.arange(ENT, dtype=jnp.int32)
    before = (e[None, :] < e[:, None])[None]
    half = du == NZ // 2
    rank = jnp.sum((before & half[:, None, :]).astype(jnp.int32), axis=2)
    up = ((du >= 1) & (du <= 3)) | (half & (rank % 2 == 0))
    down = (du >= 5) | (half & (rank % 2 == 1))
    way = up.astype(jnp.int32) + 2 * down.astype(jnp.int32)
    dist = jnp.where(down, NZ - du, du)
    order = (NZ - dist) * ENT + e[None, :]
    ahead = (way[:, None, :] == way[:, :, None]) & (order[:, None, :] < order[:, :, None])
    place = jnp.sum(ahead.astype(jnp.int32), axis=2)
    k_up = jnp.array([4, 3, 2, 1], jnp.int32)
    rel_up = jnp.stack([rel_row for rel_row in (4, 3, 2, 1)]) if False else k_up
    take = lambda a: jnp.concatenate([a[4:5], a[3:4], a[2:3], a[1:2], a[4:5], a[5:6], a[6:7], a[7:8]])
    want_way = jnp.array([1, 1, 1, 1, 2, 2, 2, 2], jnp.int32)[:, None]
    want_dist = jnp.concatenate([rel_up, k_up])[:, None]
    mine = (take(way) == want_way) & (take(dist) == want_dist)
    hit = mine[:, None, :] & (take(place)[:, None, :] == e[None, :, None])
    steps = jnp.sum(hit.astype(jnp.int32) * (take(spot)[:, None, :] + 1), axis=2) - 1
    last = jnp.stack(
        [
            way[0],
            jnp.where(way[0] == 1, place[0], 0),
            jnp.where(way[0] == 2, place[0], 0),
            jnp.where(way[0] == 0, spot[0], 0),
        ]
    )
    return jnp.concatenate([steps, last], axis=0)


def main_kernel(
    tab,
    q_hbm,
    nk_hbm,
    nv_hbm,
    kc_hbm,
    vc_hbm,
    w_hbm,
    out_ref,
    cols,
    hops,
    fins,
    kg,
    vg,
    q,
    probs,
    att,
    w_all,
    w_relay,
    y_send,
    y_recv,
    z_send,
    z_recv,
    w_send,
    w_recv,
    a_send,
    a_recv,
    local_sem,
):
    s = lax.axis_index("seq")
    t = lax.axis_index("tp")
    y, z = s // NZ, lax.rem(s, NZ)
    x, c = t // NC, lax.rem(t, NC)
    yp = lax.rem(y + 1, NY) * NZ + z
    ym = lax.rem(y + NY - 1, NY) * NZ + z
    zp = y * NZ + lax.rem(z + 1, NZ)
    zm = y * NZ + lax.rem(z + NZ - 1, NZ)
    xp = lax.rem(x + 1, NX)
    xm = lax.rem(x + NX - 1, NX)
    xo = lax.rem(x + 2, NX)
    sib = x * NC + (1 - c)

    def remote(src, dst, ssem, rsem, seq=None, tp=None):
        return pltpu.make_async_remote_copy(
            src_ref=src,
            dst_ref=dst,
            send_sem=ssem,
            recv_sem=rsem,
            device_id={"seq": s if seq is None else seq, "tp": t if tp is None else tp},
            device_id_type=MESH,
        )

    barrier = pltpu.get_barrier_semaphore()
    peers = [(yp, t), (ym, t), (zp, t), (zm, t), (s, sib)]
    peers += [(s, xx * NC + cc) for xx in (xp, xm) for cc in range(NC)]
    for ps, pt in peers:
        pl.semaphore_signal(
            barrier, inc=1, device_id={"seq": ps, "tp": pt}, device_id_type=MESH
        )

    pending = []

    locals_ = []

    def local(src, dst):
        cp = pltpu.make_async_copy(src, dst, local_sem.at[len(locals_)])
        cp.start()
        locals_.append(cp)
        return cp

    def source(ch):
        ref = kc_hbm if ch < PARTS else vc_hbm
        return ref.at[:, pl.ds((ch % PARTS) * ROWS, ROWS), :]

    own_rows = pl.ds(pl.multiple_of(y * SHARD, SHARD), SHARD)
    own_cols = [local(source(ch), cols[ch].at[own_rows]) for ch in range(CHUNKS)]
    in_q = local(q_hbm, q)
    in_nk = [local(nk_hbm.at[pl.ds(b * BLOCK, BLOCK)], kg.at[b, pl.ds(TOPB * BLOCK, BLOCK)]) for b in range(QBD)]
    in_nv = [local(nv_hbm.at[pl.ds(b * BLOCK, BLOCK)], vg.at[b, pl.ds(TOPB * BLOCK, BLOCK)]) for b in range(QBD)]

    pl.semaphore_wait(barrier, len(peers))

    half = SHARD // 2
    y_copies = []

    def y_start(ch):
        mine = [
            remote(source(ch), cols[ch].at[own_rows], y_send.at[ch, 0], y_recv.at[ch, 0], seq=yp),
            remote(source(ch), cols[ch].at[own_rows], y_send.at[ch, 1], y_recv.at[ch, 1], seq=ym),
        ]
        for cp in mine:
            cp.start()
        y_copies.append(mine)
        pending.extend(mine)

    def y_relay(ch):
        first, second = y_copies[ch]
        first.wait_recv()
        lo = pl.ds(pl.multiple_of(lax.rem(y + NY - 1, NY) * SHARD, SHARD), half)
        a = remote(cols[ch].at[lo], cols[ch].at[lo], y_send.at[ch, 2], y_recv.at[ch, 2], seq=yp)
        a.start()
        second.wait_recv()
        hi = pl.ds(pl.multiple_of(lax.rem(y + 1, NY) * SHARD + half, half), half)
        b = remote(cols[ch].at[hi], cols[ch].at[hi], y_send.at[ch, 3], y_recv.at[ch, 3], seq=ym)
        b.start()
        pending.extend([a, b])
        return a, b

    z_copies = {}
    seg = 4

    def merge(ch, d, step):
        cap = CAPS[step]
        kept = CAPS[step - 1] if step else 0
        buf = hops[d][step][ch]

        def fresh(j):
            at = tab[d * 4 + step, j]
            return at, cols[ch][jnp.maximum(at, 0)]

        def both(i, carry):
            for u in range(seg):
                j = i * seg + u
                at, new = fresh(j)
                buf[j] = jnp.where(at < 0, buf[j], new)
            return carry

        def only(i, carry):
            for u in range(seg):
                j = i * seg + u
                buf[j] = fresh(j)[1]
            return carry

        if kept:
            lax.fori_loop(0, kept // seg, both, 0)
        if cap > kept:
            lax.fori_loop(kept // seg, cap // seg, only, 0)

    def z_step(ch, step):
        for d in range(2):
            if step:
                z_copies[ch, d, step - 1].wait_recv()
            merge(ch, d, step)
            if step < 3:
                dst = hops[d][step + 1][ch].at[pl.ds(0, CAPS[step])]
            else:
                dst = fins[d][ch]
            cp = remote(
                hops[d][step][ch],
                dst,
                z_send.at[ch, d, step],
                z_recv.at[ch, d, step],
                seq=zp if d == 0 else zm,
            )
            cp.start()
            z_copies[ch, d, step] = cp
            pending.append(cp)

    def collect(ch):
        for d in range(2):
            z_copies[ch, d, 3].wait_recv()
        dst = kg if ch < PARTS else vg
        r0 = (ch % PARTS) * ROWS
        for b in range(QBD):

            def entry(i, carry):
                e = b * TOPB + i
                way = tab[8, e]
                val = jnp.where(
                    way == 0,
                    cols[ch][tab[11, e]],
                    jnp.where(way == 1, fins[0][ch][tab[9, e]], fins[1][ch][tab[10, e]]),
                )
                dst[b, pl.ds(pl.multiple_of(i * BLOCK + r0, ROWS), ROWS), :] = val
                return carry

            lax.fori_loop(0, TOPB, entry, 0)

    depth = G * HD
    width = w_hbm.shape[1] // TP
    hd = depth // 2

    def w_cols(tt):
        return pl.ds(pl.multiple_of(tt * width, width), width)

    def w_rows(tt, off=0, n=depth):
        return pl.ds(pl.multiple_of(tt * depth + off, hd), n)

    w_direct, w_first = [], []

    def w_start():
        targets = [sib] + [xx * NC + cc for xx in (xp, xm) for cc in range(NC)]
        slots = [0, 1 + c, 1 + c, 3 + c, 3 + c]
        for dirn in range(2):
            for cc in range(NC):
                cp = remote(
                    w_hbm.at[pl.ds(dirn * hd, hd), w_cols(xo * NC + cc)],
                    w_relay.at[dirn * NC + cc],
                    w_send.at[5 + dirn * NC + cc],
                    w_recv.at[5 + dirn * NC + cc],
                    tp=(xp if dirn == 0 else xm) * NC + c,
                )
                cp.start()
                w_first.append(cp)
                pending.append(cp)
        for i, (tt, slot) in enumerate(zip(targets, slots)):
            cp = remote(
                w_hbm.at[:, w_cols(tt)],
                w_all.at[w_rows(t)],
                w_send.at[i],
                w_recv.at[slot],
                tp=tt,
            )
            cp.start()
            w_direct.append(cp)
            pending.append(cp)

    w_second = []

    def w_forward():
        for dirn in range(2):
            for cc in range(NC):
                w_first[dirn * NC + cc].wait_recv()
                src_t = (xm if dirn == 0 else xp) * NC + c
                dst_t = (xp if dirn == 0 else xm) * NC + cc
                rows = w_rows(src_t, dirn * hd, hd)
                cp = remote(
                    w_relay.at[dirn * NC + cc],
                    w_all.at[rows],
                    w_send.at[9 + dirn * NC + cc],
                    w_recv.at[9 + dirn * NC + c],
                    tp=dst_t,
                )
                cp.start()
                w_second.append(cp)
                pending.append(cp)

    def w_wait():
        for slot in range(5):
            remote(
                w_hbm.at[:, w_cols(t)], w_all.at[w_rows(t)], w_send.at[0], w_recv.at[slot], tp=sib
            ).wait_recv()
        for slot in range(4):
            remote(
                w_relay.at[slot],
                w_all.at[w_rows(t, 0, hd)],
                w_send.at[9],
                w_recv.at[9 + slot],
                tp=sib,
            ).wait_recv()

    y_start(0)
    w_own = local(w_hbm.at[:, w_cols(t)], w_all.at[w_rows(t)])
    w_start()

    relays = {}

    def y_finish(ch):
        own_cols[ch].wait()
        relays[ch] = y_relay(ch)
        if ch + 1 < CHUNKS:
            y_start(ch + 1)
        for cp in relays[ch]:
            cp.wait_recv()

    def scores(b):
        rows = pl.ds(pl.multiple_of(b * BLOCK, BLOCK), BLOCK)
        keys = kg[b]
        seen = TOPB * BLOCK
        row_ids = lax.broadcasted_iota(jnp.int32, (BLOCK, BLOCK), 0)
        col_ids = lax.broadcasted_iota(jnp.int32, (BLOCK, BLOCK), 1)
        for g in range(G):
            qt = q[rows, g * HD : (g + 1) * HD]
            sc = lax.dot_general(
                qt, keys, (((1,), (1,)), ((), ())), preferred_element_type=F32
            ) * (1.0 / math.sqrt(HD))
            near = jnp.where(col_ids <= row_ids, sc[:, seen:], -1e30)
            far = sc[:, :seen]
            top = jnp.maximum(
                jnp.max(far, axis=1, keepdims=True), jnp.max(near, axis=1, keepdims=True)
            )
            ef = jnp.exp(far - top)
            en = jnp.exp(near - top)
            tot = jnp.sum(ef, axis=1, keepdims=True) + jnp.sum(en, axis=1, keepdims=True)
            inv = 1.0 / tot
            probs[b, g * BLOCK : (g + 1) * BLOCK, :seen] = (ef * inv).astype(BF16)
            probs[b, g * BLOCK : (g + 1) * BLOCK, seen:] = (en * inv).astype(BF16)

    def mix(b):
        o = jnp.dot(probs[b], vg[b], preferred_element_type=F32).astype(BF16)
        for g in range(G):
            att[t, b, :, g * HD : (g + 1) * HD] = o[g * BLOCK : (g + 1) * BLOCK]

    forwarded = False
    for wave in range(CHUNKS + 4):
        for ch in range(CHUNKS):
            step = wave - ch
            if step < 0 or step > 4:
                continue
            if step == 0:
                y_finish(ch)
            if step < 4:
                z_step(ch, step)
            else:
                collect(ch)
                if ch == PARTS - 1:
                    in_q.wait()
                    for cp in in_nk:
                        cp.wait()

                    def score_step(b, carry):
                        scores(b)
                        return carry

                    lax.fori_loop(0, QBD, score_step, 0)
        if wave == 3:
            w_forward()

    for cp in in_nv:
        cp.wait()

    hb = BLOCK // 2
    a_first, a_second, a_third = {}, {}, {}

    def sem(b, i):
        return a_send.at[b, i], a_recv.at[b, i]

    def stage_a(b):
        mix(b)
        cps = [
            remote(att.at[t, b], att.at[t, b], *sem(b, i), tp=tt)
            for i, tt in enumerate((xp * NC + c, xm * NC + c, sib))
        ]
        for cp in cps:
            cp.start()
        a_first[b] = cps
        pending.extend(cps)

    lo, hi = pl.ds(0, hb), pl.ds(hb, hb)

    def stage_b(b):
        tm, tpl = xm * NC + c, xp * NC + c
        a_first[b][0].wait_recv()
        cps = [
            remote(att.at[tm, b, lo], att.at[tm, b, lo], *sem(b, 3), tp=tpl),
            remote(att.at[tm, b], att.at[tm, b], *sem(b, 4), tp=sib),
        ]
        for cp in cps:
            cp.start()
        a_first[b][1].wait_recv()
        more = [
            remote(att.at[tpl, b, hi], att.at[tpl, b, hi], *sem(b, 5), tp=tm),
            remote(att.at[tpl, b], att.at[tpl, b], *sem(b, 6), tp=sib),
        ]
        for cp in more:
            cp.start()
        a_second[b] = cps + more
        pending.extend(a_second[b])

    def stage_c(b):
        to = xo * NC + c
        a_second[b][0].wait_recv()
        a_second[b][2].wait_recv()
        cp = remote(att.at[to, b], att.at[to, b], *sem(b, 7), tp=sib)
        cp.start()
        a_third[b] = cp
        pending.append(cp)

    def stage_d(b):
        a_first[b][2].wait_recv()
        a_second[b][1].wait_recv()
        a_second[b][3].wait_recv()
        a_third[b].wait_recv()
        acc = jnp.zeros((BLOCK, width), F32)
        for tt in range(TP):
            acc += jnp.dot(
                att[tt, b], w_all[tt * depth : (tt + 1) * depth, :], preferred_element_type=F32
            )
        out_ref[b * BLOCK : (b + 1) * BLOCK, :] = acc.astype(BF16)

    for b in range(QBD):
        stage_a(b)
    w_own.wait()
    w_wait()
    stage_b(0)
    stage_b(1)
    stage_c(0)
    stage_b(2)
    stage_c(1)
    stage_d(0)
    stage_b(3)
    stage_c(2)
    stage_d(1)
    stage_c(3)
    stage_d(2)
    stage_d(3)

    for cp in pending:
        cp.wait_send()


def exchange(table, queries, new_keys, new_values, key_cache, value_cache, out_weight):
    any_ = pl.BlockSpec(memory_space=pl.ANY)
    width = out_weight.shape[1] // TP
    blk = lambda n: pltpu.VMEM((n, ROWS, HD), BF16)
    hop_bufs = [[[blk(CAPS[i]) for _ in range(CHUNKS)] for i in range(4)] for _ in range(2)]
    fin_bufs = [[blk(CAPS[3]) for _ in range(CHUNKS)] for _ in range(2)]
    scratch = [
        [blk(NY * SHARD) for _ in range(CHUNKS)],
        hop_bufs,
        fin_bufs,
        pltpu.VMEM((QBD, (TOPB + 1) * BLOCK, HD), BF16),
        pltpu.VMEM((QBD, (TOPB + 1) * BLOCK, HD), BF16),
        pltpu.VMEM((QBD * BLOCK, G * HD), BF16),
        pltpu.VMEM((QBD, G * BLOCK, (TOPB + 1) * BLOCK), BF16),
        pltpu.VMEM((TP, QBD, BLOCK, G * HD), BF16),
        pltpu.VMEM((TP * G * HD, width), BF16),
        pltpu.VMEM((4, G * HD // 2, width), BF16),
        pltpu.SemaphoreType.DMA((CHUNKS, 4)),
        pltpu.SemaphoreType.DMA((CHUNKS, 4)),
        pltpu.SemaphoreType.DMA((CHUNKS, 2, 4)),
        pltpu.SemaphoreType.DMA((CHUNKS, 2, 4)),
        pltpu.SemaphoreType.DMA((13,)),
        pltpu.SemaphoreType.DMA((13,)),
        pltpu.SemaphoreType.DMA((QBD, 8)),
        pltpu.SemaphoreType.DMA((QBD, 8)),
        pltpu.SemaphoreType.DMA((CHUNKS + 2 + 2 * QBD,)),
    ]
    flat, tree = jax.tree.flatten(scratch)
    fixed = 8

    def kernel(*refs):
        main_kernel(*refs[:fixed], *jax.tree.unflatten(tree, refs[fixed:]))

    return pl.pallas_call(
        kernel,
        out_shape=jax.ShapeDtypeStruct((QBD * BLOCK, width), BF16),
        in_specs=[pl.BlockSpec(memory_space=pltpu.SMEM)] + [any_] * 6,
        out_specs=pl.BlockSpec(memory_space=pltpu.VMEM),
        scratch_shapes=flat,
        compiler_params=pltpu.CompilerParams(
            collective_id=1, has_side_effects=True, vmem_limit_bytes=60 * 1024 * 1024
        ),
        name="exchange",
    )(
        table,
        queries,
        new_keys,
        new_values,
        key_cache.reshape(SHARD, BLOCK, HD),
        value_cache.reshape(SHARD, BLOCK, HD),
        out_weight,
    )


def body(queries, new_keys, new_values, key_cache, value_cache, block_lists, out_weight):
    every = gather_lists(block_lists)
    table = route_tables(every)
    return exchange(table, queries, new_keys, new_values, key_cache, value_cache, out_weight)


def solution(mesh):
    in_specs = (
        P("seq", "tp"),
        P("seq", "tp"),
        P("seq", "tp"),
        P("seq", "tp"),
        P("seq", "tp"),
        P("seq", None),
        P("tp", None),
    )
    out_specs = P("seq", "tp")
    return jax.shard_map(body, mesh=mesh, in_specs=in_specs, out_specs=out_specs, check_vma=False)
```

```python
import functools
import math

import jax
import jax.numpy as jnp
from jax import lax
from jax.experimental import pallas as pl
from jax.experimental.pallas import tpu as pltpu
from jax.sharding import PartitionSpec as P

HD = 128
BLOCK = 128
TOPB = 8
NY, NZ, NX, NC = 4, 8, 4, 2
SEQ = NY * NZ
TP = NX * NC
SHARD = 32
QBD = 4
ENT = QBD * TOPB
G = 4
LEVELS = ((8, 14, 18, 22), (8, 16, 24, 28), (8, 24, 32, 32))
SPLIT = 8
PARTS = 4
ROWS = BLOCK // PARTS
CHUNKS = 2 * PARTS
MESH = pl.DeviceIdType.MESH
F32 = jnp.float32
BF16 = jnp.bfloat16


def plan(caps):
    slot, direct, merge, hop = 1.31 / CHUNKS, 42.0 / CHUNKS, 0.04, 1.5
    ready = {("z", 0, 0): 1.0, ("ya", 1): direct + hop}
    now, link, order = 0.0, 0.0, []
    while ready:
        rank = {"ya": 0, "yb": 0, "z": 1, "f": 2, "s": 3}
        due = [k for k in ready if ready[k] <= now]
        if due:
            step = min(due, key=lambda k: (rank[k[0]], -k[2] if k[0] == "z" else 0, k[1:]))
        else:
            step = min(ready, key=lambda k: (ready[k], rank[k[0]], k[1:]))
        now = max(now, ready.pop(step))
        order.append(step)
        kind, ch = step[:2]
        if kind == "ya":
            ready["yb", ch] = now + direct / 2 + hop
        elif kind == "yb":
            if ch + 1 < CHUNKS:
                ready["ya", ch + 1] = now + direct + hop
            ready["z", ch, 0] = now
        elif kind == "z":
            now += 2 * caps[step[2]] * merge / PARTS
            link = max(link, now) + caps[step[2]] * slot
            ready[("z", ch, step[2] + 1) if step[2] < 3 else ("f", ch)] = link + hop
        elif kind == "f":
            now += 1.0
            if ch == PARTS - 1:
                for b in range(QBD):
                    ready["s", b] = now
        else:
            now += 1.5
    return order


def total(mask, axis):
    return jnp.sum(jnp.where(mask, 1, 0), axis=axis, keepdims=True)


def prepare_kernel(
    lists, kc_hbm, cols_out, tab_out, level_out, every, levels, l_send, l_recv, v_send, v_recv, y_send, y_recv, sem
):
    s = lax.axis_index("seq")
    y, z = s // NZ, lax.rem(s, NZ)
    yp = lax.rem(y + 1, NY)
    ym = lax.rem(y + NY - 1, NY)

    barrier = pltpu.get_barrier_semaphore()
    ring_z = [y * NZ + lax.rem(z + i, NZ) for i in range(1, NZ)]
    ring_y = [lax.rem(y + i, NY) * NZ + z for i in range(1, NY)]
    for peer in ring_z + ring_y:
        pl.semaphore_signal(barrier, inc=1, device_id={"seq": peer}, device_id_type=MESH)

    own_rows = pl.ds(pl.multiple_of(y * SHARD, SHARD), SHARD)
    mine = kc_hbm.at[:, pl.ds(0, ROWS), :]
    keep = pltpu.make_async_copy(mine, cols_out.at[own_rows], sem.at[0])
    keep.start()
    every[z] = lists[...]
    pl.semaphore_wait(barrier, NZ + NY - 2)

    def remote(src, dst, ssem, rsem, seq):
        return pltpu.make_async_remote_copy(
            src_ref=src,
            dst_ref=dst,
            send_sem=ssem,
            recv_sem=rsem,
            device_id={"seq": seq},
            device_id_type=MESH,
        )

    told = [
        remote(lists, every.at[z], l_send.at[i], l_recv.at[i], peer) for i, peer in enumerate(ring_z)
    ]
    for cp in told:
        cp.start()
    direct = [
        remote(mine, cols_out.at[own_rows], y_send.at[i], y_recv.at[i], seq * NZ + z)
        for i, seq in enumerate((yp, ym))
    ]
    for cp in direct:
        cp.start()
    for cp in told:
        cp.wait_recv()

    shape = (ENT, 128)
    e_col = lax.broadcasted_iota(jnp.int32, shape, 0)
    e_row = lax.broadcasted_iota(jnp.int32, shape, 1)
    valid = e_row < ENT
    need = jnp.zeros((1, 1), jnp.int32)
    for k in range(NZ):
        zk = lax.rem(z + k, NZ)
        col = every[zk, :ENT]
        row = jnp.broadcast_to(every[zk, ENT : ENT + 1], shape)
        spot_col = (col >> 8) * SHARD + (col & (SHARD - 1))
        du_col = (zk - ((col >> 5) & (NZ - 1))) & (NZ - 1)
        du_row = (zk - ((row >> 5) & (NZ - 1))) & (NZ - 1)
        n_up = total((du_row >= 1) & (du_row <= 3) & valid, 1)[:1]
        n_down = total((du_row >= 5) & valid, 1)[:1]
        n_half = total((du_row == 4) & valid, 1)[:1]
        share = (n_half + n_down - n_up + 1) >> 1
        share = jnp.minimum(jnp.maximum(share, n_half - SPLIT), jnp.minimum(n_half, SPLIT))
        share = jnp.maximum(share, 0)
        rank_col = total((e_row < e_col) & (du_row == 4) & valid, 1)
        rank_row = total((e_col < e_row) & (du_col == 4), 0)

        def routed(du, rank, bad):
            first = rank < share
            up = ((du >= 1) & (du <= 3)) | ((du == 4) & first)
            down = (du >= 5) | ((du == 4) & jnp.logical_not(first))
            way = jnp.where(up, 1, jnp.where(down, 2, 0))
            way = jnp.where(bad, 3, way)
            dist = jnp.where(down, NZ - du, du)
            return way, dist

        way_col, dist_col = routed(du_col, rank_col, e_row < 0)
        way_row, dist_row = routed(du_row, rank_row, jnp.logical_not(valid))
        order_col = (NZ - dist_col) * ENT + e_col
        order_row = (NZ - dist_row) * ENT + e_row
        same = way_col == way_row
        place_col = total(same & (order_row < order_col), 1)

        for i in range(4):
            for way in (1, 2):
                count = total((way_row == way) & (dist_row >= 4 - i), 1)[:1]
                for level in range(len(LEVELS) - 1):
                    over = jnp.where(count > LEVELS[level][i], level + 1, 0)
                    need = jnp.maximum(need, over)

        def pick(way, dist):
            hit = (way_col == way) & (dist_col == dist) & (place_col == e_row)
            return jnp.sum(jnp.where(hit, spot_col + 1, 0), axis=0, keepdims=True) - 1

        if 1 <= k <= 4:
            tab_out[4 - k : 5 - k, :] = pick(1, k)
        if k >= 4:
            tab_out[k : k + 1, :] = pick(2, NZ - k)
        if k == 0:
            place_row = total(same & (order_col < order_row), 0)
            way = way_row[:1]
            spot = ((row >> 8) * SHARD + (row & (SHARD - 1)))[:1]
            tab_out[8:9, :] = way
            tab_out[9:10, :] = jnp.where(way == 1, place_row, 0)
            tab_out[10:11, :] = jnp.where(way == 2, place_row, 0)
            tab_out[11:12, :] = jnp.where(way == 0, spot, 0)
            tab_out[12:16, :] = jnp.zeros((4, 128), jnp.int32)

    levels[y] = jnp.broadcast_to(need, (8, 128))
    agree = [
        remote(levels.at[y], levels.at[y], v_send.at[i], v_recv.at[i], peer)
        for i, peer in enumerate(ring_y)
    ]
    for cp in agree:
        cp.start()

    half = SHARD // 2
    lo = pl.ds(pl.multiple_of(ym * SHARD, SHARD), half)
    hi = pl.ds(pl.multiple_of(yp * SHARD + half, half), half)
    direct[0].wait_recv()
    relay_up = remote(cols_out.at[lo], cols_out.at[lo], y_send.at[2], y_recv.at[2], yp * NZ + z)
    relay_up.start()
    direct[1].wait_recv()
    relay_down = remote(cols_out.at[hi], cols_out.at[hi], y_send.at[3], y_recv.at[3], ym * NZ + z)
    relay_down.start()

    for cp in agree:
        cp.wait_recv()
    level_out[...] = jnp.maximum(
        jnp.maximum(levels[0], levels[1]), jnp.maximum(levels[2], levels[3])
    )
    relay_up.wait_recv()
    relay_down.wait_recv()
    keep.wait()
    for cp in told + direct + agree + [relay_up, relay_down]:
        cp.wait_send()


def prepare(block_lists, key_blocks):
    flat = block_lists.reshape(ENT)
    col = jnp.broadcast_to(flat[:, None], (ENT, 128))
    row = jnp.broadcast_to(jnp.pad(flat, (0, 128 - ENT))[None], (8, 128))
    lists = jnp.concatenate([col, row], axis=0)
    dma = pltpu.SemaphoreType.DMA
    vmem = pl.BlockSpec(memory_space=pltpu.VMEM)
    any_ = pl.BlockSpec(memory_space=pl.ANY)
    return pl.pallas_call(
        prepare_kernel,
        out_shape=(
            jax.ShapeDtypeStruct((NY * SHARD, ROWS, HD), BF16),
            jax.ShapeDtypeStruct((16, 128), jnp.int32),
            jax.ShapeDtypeStruct((8, 128), jnp.int32),
        ),
        in_specs=[vmem, any_],
        out_specs=(any_, vmem, vmem),
        scratch_shapes=[
            pltpu.VMEM((NZ, ENT + 8, 128), jnp.int32),
            pltpu.VMEM((NY, 8, 128), jnp.int32),
            dma((NZ - 1,)),
            dma((NZ - 1,)),
            dma((NY - 1,)),
            dma((NY - 1,)),
            dma((4,)),
            dma((4,)),
            dma((1,)),
        ],
        compiler_params=pltpu.CompilerParams(collective_id=0, has_side_effects=True),
        name="prepare",
    )(lists, key_blocks)


def main_kernel(
    caps,
    tab,
    first_hbm,
    q_hbm,
    nk_hbm,
    nv_hbm,
    kc_hbm,
    vc_hbm,
    w_hbm,
    out_ref,
    cols,
    hops,
    fins,
    kg,
    vg,
    q,
    probs,
    att,
    w_all,
    w_relay,
    y_send,
    y_recv,
    z_send,
    z_recv,
    w_send,
    w_recv,
    a_send,
    a_recv,
    local_sem,
):
    s = lax.axis_index("seq")
    t = lax.axis_index("tp")
    y, z = s // NZ, lax.rem(s, NZ)
    x, c = t // NC, lax.rem(t, NC)
    yp = lax.rem(y + 1, NY) * NZ + z
    ym = lax.rem(y + NY - 1, NY) * NZ + z
    zp = y * NZ + lax.rem(z + 1, NZ)
    zm = y * NZ + lax.rem(z + NZ - 1, NZ)
    xp = lax.rem(x + 1, NX)
    xm = lax.rem(x + NX - 1, NX)
    xo = lax.rem(x + 2, NX)
    sib = x * NC + (1 - c)

    def remote(src, dst, ssem, rsem, seq=None, tp=None):
        return pltpu.make_async_remote_copy(
            src_ref=src,
            dst_ref=dst,
            send_sem=ssem,
            recv_sem=rsem,
            device_id={"seq": s if seq is None else seq, "tp": t if tp is None else tp},
            device_id_type=MESH,
        )

    barrier = pltpu.get_barrier_semaphore()
    peers = [(yp, t), (ym, t), (zp, t), (zm, t), (s, sib)]
    peers += [(s, xx * NC + cc) for xx in (xp, xm) for cc in range(NC)]
    for ps, pt in peers:
        pl.semaphore_signal(
            barrier, inc=1, device_id={"seq": ps, "tp": pt}, device_id_type=MESH
        )

    pending = []

    locals_ = []

    def local(src, dst):
        cp = pltpu.make_async_copy(src, dst, local_sem.at[len(locals_)])
        cp.start()
        locals_.append(cp)
        return cp

    def source(ch):
        ref = kc_hbm if ch < PARTS else vc_hbm
        return ref.at[:, pl.ds((ch % PARTS) * ROWS, ROWS), :]

    own_rows = pl.ds(pl.multiple_of(y * SHARD, SHARD), SHARD)
    own_cols = [local(first_hbm, cols[0])]
    own_cols += [local(source(ch), cols[ch].at[own_rows]) for ch in range(1, CHUNKS)]
    in_q = local(q_hbm, q)
    in_nk = [local(nk_hbm.at[pl.ds(b * BLOCK, BLOCK)], kg.at[b, pl.ds(TOPB * BLOCK, BLOCK)]) for b in range(QBD)]
    in_nv = [local(nv_hbm.at[pl.ds(b * BLOCK, BLOCK)], vg.at[b, pl.ds(TOPB * BLOCK, BLOCK)]) for b in range(QBD)]

    pl.semaphore_wait(barrier, len(peers))

    half = SHARD // 2
    y_copies = {}

    def y_start(ch):
        mine = [
            remote(source(ch), cols[ch].at[own_rows], y_send.at[ch, 0], y_recv.at[ch, 0], seq=yp),
            remote(source(ch), cols[ch].at[own_rows], y_send.at[ch, 1], y_recv.at[ch, 1], seq=ym),
        ]
        for cp in mine:
            cp.start()
        y_copies[ch] = mine
        pending.extend(mine)

    def y_relay(ch):
        first, second = y_copies[ch]
        first.wait_recv()
        lo = pl.ds(pl.multiple_of(lax.rem(y + NY - 1, NY) * SHARD, SHARD), half)
        a = remote(cols[ch].at[lo], cols[ch].at[lo], y_send.at[ch, 2], y_recv.at[ch, 2], seq=yp)
        a.start()
        second.wait_recv()
        hi = pl.ds(pl.multiple_of(lax.rem(y + 1, NY) * SHARD + half, half), half)
        b = remote(cols[ch].at[hi], cols[ch].at[hi], y_send.at[ch, 3], y_recv.at[ch, 3], seq=ym)
        b.start()
        pending.extend([a, b])
        return a, b

    z_copies = {}
    seg = 2

    def merge(ch, d, step):
        cap = caps[step]
        kept = caps[step - 1] if step else 0
        buf = hops[d][step][ch]

        def fresh(j):
            at = tab[d * 4 + step, j]
            return at, cols[ch][jnp.maximum(at, 0)]

        def both(i, carry):
            for u in range(seg):
                j = i * seg + u
                at, new = fresh(j)
                buf[j] = jnp.where(at < 0, buf[j], new)
            return carry

        def only(i, carry):
            for u in range(seg):
                j = i * seg + u
                buf[j] = fresh(j)[1]
            return carry

        if kept:
            lax.fori_loop(0, kept // seg, both, 0)
        if cap > kept:
            lax.fori_loop(kept // seg, cap // seg, only, 0)

    def z_step(ch, step):
        if ch == 0 and step == 0:
            own_cols[0].wait()
        for d in range(2):
            if step:
                z_copies[ch, d, step - 1].wait_recv()
            merge(ch, d, step)
            if step < 3:
                dst = hops[d][step + 1][ch].at[pl.ds(0, caps[step])]
            else:
                dst = fins[d][ch]
            cp = remote(
                hops[d][step][ch],
                dst,
                z_send.at[ch, d, step],
                z_recv.at[ch, d, step],
                seq=zp if d == 0 else zm,
            )
            cp.start()
            z_copies[ch, d, step] = cp
            pending.append(cp)

    def collect(ch):
        for d in range(2):
            z_copies[ch, d, 3].wait_recv()
        dst = kg if ch < PARTS else vg
        r0 = (ch % PARTS) * ROWS
        for b in range(QBD):

            def entry(i, carry):
                e = b * TOPB + i
                way = tab[8, e]
                val = jnp.where(
                    way == 0,
                    cols[ch][tab[11, e]],
                    jnp.where(way == 1, fins[0][ch][tab[9, e]], fins[1][ch][tab[10, e]]),
                )
                dst[b, pl.ds(pl.multiple_of(i * BLOCK + r0, ROWS), ROWS), :] = val
                return carry

            lax.fori_loop(0, TOPB, entry, 0)

    depth = G * HD
    width = w_hbm.shape[1] // TP
    hd = depth // 2

    def w_cols(tt):
        return pl.ds(pl.multiple_of(tt * width, width), width)

    def w_rows(tt, off=0, n=depth):
        return pl.ds(pl.multiple_of(tt * depth + off, hd), n)

    w_direct, w_first = [], []

    def w_start():
        targets = [sib] + [xx * NC + cc for xx in (xp, xm) for cc in range(NC)]
        slots = [0, 1 + c, 1 + c, 3 + c, 3 + c]
        for dirn in range(2):
            for cc in range(NC):
                cp = remote(
                    w_hbm.at[pl.ds(dirn * hd, hd), w_cols(xo * NC + cc)],
                    w_relay.at[dirn * NC + cc],
                    w_send.at[5 + dirn * NC + cc],
                    w_recv.at[5 + dirn * NC + cc],
                    tp=(xp if dirn == 0 else xm) * NC + c,
                )
                cp.start()
                w_first.append(cp)
                pending.append(cp)
        for i, (tt, slot) in enumerate(zip(targets, slots)):
            cp = remote(
                w_hbm.at[:, w_cols(tt)],
                w_all.at[w_rows(t)],
                w_send.at[i],
                w_recv.at[slot],
                tp=tt,
            )
            cp.start()
            w_direct.append(cp)
            pending.append(cp)

    w_second = []

    def w_forward():
        for dirn in range(2):
            for cc in range(NC):
                w_first[dirn * NC + cc].wait_recv()
                src_t = (xm if dirn == 0 else xp) * NC + c
                dst_t = (xp if dirn == 0 else xm) * NC + cc
                rows = w_rows(src_t, dirn * hd, hd)
                cp = remote(
                    w_relay.at[dirn * NC + cc],
                    w_all.at[rows],
                    w_send.at[9 + dirn * NC + cc],
                    w_recv.at[9 + dirn * NC + c],
                    tp=dst_t,
                )
                cp.start()
                w_second.append(cp)
                pending.append(cp)

    def w_wait():
        for slot in range(5):
            remote(
                w_hbm.at[:, w_cols(t)], w_all.at[w_rows(t)], w_send.at[0], w_recv.at[slot], tp=sib
            ).wait_recv()
        for slot in range(4):
            remote(
                w_relay.at[slot],
                w_all.at[w_rows(t, 0, hd)],
                w_send.at[9],
                w_recv.at[9 + slot],
                tp=sib,
            ).wait_recv()

    y_start(1)
    w_own = local(w_hbm.at[:, w_cols(t)], w_all.at[w_rows(t)])
    w_start()

    relays = {}

    def y_first(ch):
        own_cols[ch].wait()
        relays[ch] = y_relay(ch)

    def y_second(ch):
        for cp in relays[ch]:
            cp.wait_recv()
        if ch + 1 < CHUNKS:
            y_start(ch + 1)

    def scores(b):
        rows = pl.ds(pl.multiple_of(b * BLOCK, BLOCK), BLOCK)
        keys = kg[b]
        seen = TOPB * BLOCK
        row_ids = lax.broadcasted_iota(jnp.int32, (BLOCK, BLOCK), 0)
        col_ids = lax.broadcasted_iota(jnp.int32, (BLOCK, BLOCK), 1)

        def head(g, carry):
            lanes = pl.ds(pl.multiple_of(g * HD, HD), HD)
            out = pl.ds(pl.multiple_of(g * BLOCK, BLOCK), BLOCK)
            sc = lax.dot_general(
                q[rows, lanes], keys, (((1,), (1,)), ((), ())), preferred_element_type=F32
            ) * (1.0 / math.sqrt(HD))
            near = jnp.where(col_ids <= row_ids, sc[:, seen:], -1e30)
            far = sc[:, :seen]
            top = jnp.maximum(
                jnp.max(far, axis=1, keepdims=True), jnp.max(near, axis=1, keepdims=True)
            )
            ef = jnp.exp(far - top)
            en = jnp.exp(near - top)
            tot = jnp.sum(ef, axis=1, keepdims=True) + jnp.sum(en, axis=1, keepdims=True)
            inv = 1.0 / tot
            probs[b, out, :seen] = (ef * inv).astype(BF16)
            probs[b, out, seen:] = (en * inv).astype(BF16)
            return carry

        lax.fori_loop(0, G, head, 0)

    def mix(b):
        o = jnp.dot(probs[b], vg[b], preferred_element_type=F32).astype(BF16)
        for g in range(G):
            att[t, b, :, g * HD : (g + 1) * HD] = o[g * BLOCK : (g + 1) * BLOCK]

    seen_scores = 0
    for step in plan(caps):
        kind, ch = step[:2]
        if kind == "ya":
            y_first(ch)
        elif kind == "yb":
            y_second(ch)
            if ch == CHUNKS - 1:
                w_forward()
        elif kind == "z":
            z_step(ch, step[2])
        elif kind == "f":
            collect(ch)
        else:
            if not seen_scores:
                in_q.wait()
                for cp in in_nk:
                    cp.wait()
            seen_scores += 1
            scores(ch)

    for cp in in_nv:
        cp.wait()

    hb = BLOCK // 2
    a_first, a_second, a_third = {}, {}, {}

    def sem(b, i):
        return a_send.at[b, i], a_recv.at[b, i]

    def stage_a(b):
        mix(b)
        cps = [
            remote(att.at[t, b], att.at[t, b], *sem(b, i), tp=tt)
            for i, tt in enumerate((xp * NC + c, xm * NC + c, sib))
        ]
        for cp in cps:
            cp.start()
        a_first[b] = cps
        pending.extend(cps)

    lo, hi = pl.ds(0, hb), pl.ds(hb, hb)

    def stage_b(b):
        tm, tpl = xm * NC + c, xp * NC + c
        a_first[b][0].wait_recv()
        cps = [
            remote(att.at[tm, b, lo], att.at[tm, b, lo], *sem(b, 3), tp=tpl),
            remote(att.at[tm, b], att.at[tm, b], *sem(b, 4), tp=sib),
        ]
        for cp in cps:
            cp.start()
        a_first[b][1].wait_recv()
        more = [
            remote(att.at[tpl, b, hi], att.at[tpl, b, hi], *sem(b, 5), tp=tm),
            remote(att.at[tpl, b], att.at[tpl, b], *sem(b, 6), tp=sib),
        ]
        for cp in more:
            cp.start()
        a_second[b] = cps + more
        pending.extend(a_second[b])

    def stage_c(b):
        to = xo * NC + c
        a_second[b][0].wait_recv()
        a_second[b][2].wait_recv()
        cp = remote(att.at[to, b], att.at[to, b], *sem(b, 7), tp=sib)
        cp.start()
        a_third[b] = cp
        pending.append(cp)

    def stage_d(b):
        a_first[b][2].wait_recv()
        a_second[b][1].wait_recv()
        a_second[b][3].wait_recv()
        a_third[b].wait_recv()
        acc = jnp.zeros((BLOCK, width), F32)
        for tt in range(TP):
            acc += jnp.dot(
                att[tt, b], w_all[tt * depth : (tt + 1) * depth, :], preferred_element_type=F32
            )
        out_ref[b * BLOCK : (b + 1) * BLOCK, :] = acc.astype(BF16)

    for b in range(QBD):
        stage_a(b)
    w_own.wait()
    w_wait()
    stage_b(0)
    stage_b(1)
    stage_c(0)
    stage_b(2)
    stage_c(1)
    stage_d(0)
    stage_b(3)
    stage_c(2)
    stage_d(1)
    stage_c(3)
    stage_d(2)
    stage_d(3)

    for cp in pending:
        cp.wait_send()


def exchange(level, table, first, queries, new_keys, new_values, key_cache, value_cache, out_weight):
    caps = LEVELS[level]
    any_ = pl.BlockSpec(memory_space=pl.ANY)
    width = out_weight.shape[1] // TP
    blk = lambda n: pltpu.VMEM((n, ROWS, HD), BF16)
    hop_bufs = [[[blk(caps[i]) for _ in range(CHUNKS)] for i in range(4)] for _ in range(2)]
    fin_bufs = [[blk(caps[3]) for _ in range(CHUNKS)] for _ in range(2)]
    scratch = [
        [blk(NY * SHARD) for _ in range(CHUNKS)],
        hop_bufs,
        fin_bufs,
        pltpu.VMEM((QBD, (TOPB + 1) * BLOCK, HD), BF16),
        pltpu.VMEM((QBD, (TOPB + 1) * BLOCK, HD), BF16),
        pltpu.VMEM((QBD * BLOCK, G * HD), BF16),
        pltpu.VMEM((QBD, G * BLOCK, (TOPB + 1) * BLOCK), BF16),
        pltpu.VMEM((TP, QBD, BLOCK, G * HD), BF16),
        pltpu.VMEM((TP * G * HD, width), BF16),
        pltpu.VMEM((4, G * HD // 2, width), BF16),
        pltpu.SemaphoreType.DMA((CHUNKS, 4)),
        pltpu.SemaphoreType.DMA((CHUNKS, 4)),
        pltpu.SemaphoreType.DMA((CHUNKS, 2, 4)),
        pltpu.SemaphoreType.DMA((CHUNKS, 2, 4)),
        pltpu.SemaphoreType.DMA((13,)),
        pltpu.SemaphoreType.DMA((13,)),
        pltpu.SemaphoreType.DMA((QBD, 8)),
        pltpu.SemaphoreType.DMA((QBD, 8)),
        pltpu.SemaphoreType.DMA((CHUNKS + 2 + 2 * QBD,)),
    ]
    flat, tree = jax.tree.flatten(scratch)
    fixed = 9

    def kernel(*refs):
        main_kernel(caps, *refs[:fixed], *jax.tree.unflatten(tree, refs[fixed:]))

    return pl.pallas_call(
        kernel,
        out_shape=jax.ShapeDtypeStruct((QBD * BLOCK, width), BF16),
        in_specs=[pl.BlockSpec(memory_space=pltpu.SMEM)] + [any_] * 7,
        out_specs=pl.BlockSpec(memory_space=pltpu.VMEM),
        scratch_shapes=flat,
        compiler_params=pltpu.CompilerParams(
            collective_id=1 + level, has_side_effects=True, vmem_limit_bytes=60 * 1024 * 1024
        ),
        name="exchange",
    )(
        table,
        first,
        queries,
        new_keys,
        new_values,
        key_cache,
        value_cache,
        out_weight,
    )


def body(queries, new_keys, new_values, key_cache, value_cache, block_lists, out_weight):
    key_blocks = key_cache.reshape(SHARD, BLOCK, HD)
    value_blocks = value_cache.reshape(SHARD, BLOCK, HD)
    first, table, level = prepare(block_lists, key_blocks)
    branches = [functools.partial(exchange, i) for i in range(len(LEVELS))]
    return lax.switch(
        level[0, 0],
        branches,
        table,
        first,
        queries,
        new_keys,
        new_values,
        key_blocks,
        value_blocks,
        out_weight,
    )


def solution(mesh):
    in_specs = (
        P("seq", "tp"),
        P("seq", "tp"),
        P("seq", "tp"),
        P("seq", "tp"),
        P("seq", "tp"),
        P("seq", None),
        P("tp", None),
    )
    out_specs = P("seq", "tp")
    return jax.shard_map(body, mesh=mesh, in_specs=in_specs, out_specs=out_specs, check_vma=False)
```

```python
import functools
import math

import jax
import jax.numpy as jnp
from jax import lax
from jax.experimental import pallas as pl
from jax.experimental.pallas import tpu as pltpu
from jax.sharding import PartitionSpec as P

HD = 128
BLOCK = 128
TOPB = 8
NY, NZ, NX, NC = 4, 8, 4, 2
SEQ = NY * NZ
TP = NX * NC
SHARD = 32
QBD = 4
ENT = QBD * TOPB
G = 4
LEVELS = ((8, 14, 18, 22), (8, 16, 24, 28), (8, 24, 32, 32))
SPLIT = 8
PARTS = 4
ROWS = BLOCK // PARTS
CHUNKS = 2 * PARTS
MESH = pl.DeviceIdType.MESH
F32 = jnp.float32
BF16 = jnp.bfloat16


ORDER = (
    ("z", 0, 0),
    ("v", 0),
    ("z", 0, 1),
    ("v", 1),
    ("v", 2),
    ("ya", 1),
    ("yb", 1),
    ("z", 1, 0),
    ("z", 0, 2),
    ("ya", 2),
    ("v", 3),
    ("z", 0, 3),
    ("yb", 2),
    ("z", 2, 0),
    ("z", 1, 1),
    ("z", 2, 1),
    ("ya", 3),
    ("f", 0),
    ("z", 1, 2),
    ("yb", 3),
    ("z", 3, 0),
    ("z", 2, 2),
    ("z", 3, 1),
    ("ya", 4),
    ("z", 2, 3),
    ("yb", 4),
    ("z", 1, 3),
    ("z", 4, 0),
    ("f", 2),
    ("z", 3, 2),
    ("ya", 5),
    ("z", 4, 1),
    ("f", 1),
    ("yb", 5),
    ("z", 5, 0),
    ("z", 3, 3),
    ("z", 5, 1),
    ("ya", 6),
    ("z", 4, 2),
    ("f", 3),
    ("s", 0),
    ("yb", 6),
    ("z", 6, 0),
    ("z", 5, 2),
    ("z", 6, 1),
    ("ya", 7),
    ("z", 4, 3),
    ("s", 1),
    ("yb", 7),
    ("z", 7, 0),
    ("z", 5, 3),
    ("z", 7, 1),
    ("s", 2),
    ("z", 6, 2),
    ("f", 4),
    ("s", 3),
    ("f", 5),
    ("z", 7, 2),
    ("A", 0, 0),
    ("z", 6, 3),
    ("A", 0, 1),
    ("A", 0, 2),
    ("B", 0, 0),
    ("z", 7, 3),
    ("A", 0, 3),
    ("B", 0, 1),
    ("f", 6),
    ("B", 0, 3),
    ("C", 0, 0),
    ("C", 0, 1),
    ("B", 0, 2),
    ("f", 7),
    ("A", 1, 0),
    ("A", 1, 1),
    ("A", 1, 2),
    ("A", 1, 3),
    ("D", 0, 1),
    ("B", 1, 0),
    ("C", 0, 2),
    ("B", 1, 1),
    ("D", 0, 0),
    ("B", 1, 2),
    ("C", 0, 3),
    ("B", 1, 3),
    ("C", 1, 0),
    ("C", 1, 1),
    ("D", 0, 2),
    ("C", 1, 2),
    ("D", 0, 3),
    ("C", 1, 3),
    ("D", 1, 0),
    ("D", 1, 1),
    ("D", 1, 2),
    ("D", 1, 3),
)


def total(mask, axis):
    return jnp.sum(jnp.where(mask, 1, 0), axis=axis, keepdims=True)


def prepare_kernel(
    lists, kc_hbm, cols_out, tab_out, level_out, every, levels, l_send, l_recv, v_send, v_recv, y_send, y_recv, sem
):
    s = lax.axis_index("seq")
    y, z = s // NZ, lax.rem(s, NZ)
    yp = lax.rem(y + 1, NY)
    ym = lax.rem(y + NY - 1, NY)

    barrier = pltpu.get_barrier_semaphore()
    ring_z = [y * NZ + lax.rem(z + i, NZ) for i in range(1, NZ)]
    ring_y = [lax.rem(y + i, NY) * NZ + z for i in range(1, NY)]
    for peer in ring_z + ring_y:
        pl.semaphore_signal(barrier, inc=1, device_id={"seq": peer}, device_id_type=MESH)

    own_rows = pl.ds(pl.multiple_of(y * SHARD, SHARD), SHARD)
    mine = kc_hbm.at[:, pl.ds(0, ROWS), :]
    keep = pltpu.make_async_copy(mine, cols_out.at[own_rows], sem.at[0])
    keep.start()
    every[z] = lists[...]
    pl.semaphore_wait(barrier, NZ + NY - 2)

    def remote(src, dst, ssem, rsem, seq):
        return pltpu.make_async_remote_copy(
            src_ref=src,
            dst_ref=dst,
            send_sem=ssem,
            recv_sem=rsem,
            device_id={"seq": seq},
            device_id_type=MESH,
        )

    told = [
        remote(lists, every.at[z], l_send.at[i], l_recv.at[i], peer) for i, peer in enumerate(ring_z)
    ]
    for cp in told:
        cp.start()
    direct = [
        remote(mine, cols_out.at[own_rows], y_send.at[i], y_recv.at[i], seq * NZ + z)
        for i, seq in enumerate((yp, ym))
    ]
    for cp in direct:
        cp.start()
    for cp in told:
        cp.wait_recv()

    shape = (ENT, 128)
    e_col = lax.broadcasted_iota(jnp.int32, shape, 0)
    e_row = lax.broadcasted_iota(jnp.int32, shape, 1)
    valid = e_row < ENT
    need = jnp.zeros((1, 1), jnp.int32)
    for k in range(NZ):
        zk = lax.rem(z + k, NZ)
        col = every[zk, :ENT]
        row = jnp.broadcast_to(every[zk, ENT : ENT + 1], shape)
        spot_col = (col >> 8) * SHARD + (col & (SHARD - 1))
        du_col = (zk - ((col >> 5) & (NZ - 1))) & (NZ - 1)
        du_row = (zk - ((row >> 5) & (NZ - 1))) & (NZ - 1)
        n_up = total((du_row >= 1) & (du_row <= 3) & valid, 1)[:1]
        n_down = total((du_row >= 5) & valid, 1)[:1]
        n_half = total((du_row == 4) & valid, 1)[:1]
        share = (n_half + n_down - n_up + 1) >> 1
        share = jnp.minimum(jnp.maximum(share, n_half - SPLIT), jnp.minimum(n_half, SPLIT))
        share = jnp.maximum(share, 0)
        rank_col = total((e_row < e_col) & (du_row == 4) & valid, 1)
        rank_row = total((e_col < e_row) & (du_col == 4), 0)

        def routed(du, rank, bad):
            first = rank < share
            up = ((du >= 1) & (du <= 3)) | ((du == 4) & first)
            down = (du >= 5) | ((du == 4) & jnp.logical_not(first))
            way = jnp.where(up, 1, jnp.where(down, 2, 0))
            way = jnp.where(bad, 3, way)
            dist = jnp.where(down, NZ - du, du)
            return way, dist

        way_col, dist_col = routed(du_col, rank_col, e_row < 0)
        way_row, dist_row = routed(du_row, rank_row, jnp.logical_not(valid))
        order_col = (NZ - dist_col) * ENT + e_col
        order_row = (NZ - dist_row) * ENT + e_row
        same = way_col == way_row
        place_col = total(same & (order_row < order_col), 1)

        for i in range(4):
            for way in (1, 2):
                count = total((way_row == way) & (dist_row >= 4 - i), 1)[:1]
                for level in range(len(LEVELS) - 1):
                    over = jnp.where(count > LEVELS[level][i], level + 1, 0)
                    need = jnp.maximum(need, over)

        def pick(way, dist):
            hit = (way_col == way) & (dist_col == dist) & (place_col == e_row)
            return jnp.sum(jnp.where(hit, spot_col + 1, 0), axis=0, keepdims=True) - 1

        if 1 <= k <= 4:
            tab_out[4 - k : 5 - k, :] = pick(1, k)
        if k >= 4:
            tab_out[k : k + 1, :] = pick(2, NZ - k)
        if k == 0:
            place_row = total(same & (order_col < order_row), 0)
            way = way_row[:1]
            spot = ((row >> 8) * SHARD + (row & (SHARD - 1)))[:1]
            tab_out[8:9, :] = way
            tab_out[9:10, :] = jnp.where(way == 1, place_row, 0)
            tab_out[10:11, :] = jnp.where(way == 2, place_row, 0)
            tab_out[11:12, :] = jnp.where(way == 0, spot, 0)
            tab_out[12:16, :] = jnp.zeros((4, 128), jnp.int32)

    levels[y] = jnp.broadcast_to(need, (8, 128))
    agree = [
        remote(levels.at[y], levels.at[y], v_send.at[i], v_recv.at[i], peer)
        for i, peer in enumerate(ring_y)
    ]
    for cp in agree:
        cp.start()

    half = SHARD // 2
    lo = pl.ds(pl.multiple_of(ym * SHARD, SHARD), half)
    hi = pl.ds(pl.multiple_of(yp * SHARD + half, half), half)
    direct[0].wait_recv()
    relay_up = remote(cols_out.at[lo], cols_out.at[lo], y_send.at[2], y_recv.at[2], yp * NZ + z)
    relay_up.start()
    direct[1].wait_recv()
    relay_down = remote(cols_out.at[hi], cols_out.at[hi], y_send.at[3], y_recv.at[3], ym * NZ + z)
    relay_down.start()

    for cp in agree:
        cp.wait_recv()
    level_out[...] = jnp.maximum(
        jnp.maximum(levels[0], levels[1]), jnp.maximum(levels[2], levels[3])
    )
    relay_up.wait_recv()
    relay_down.wait_recv()
    keep.wait()
    for cp in told + direct + agree + [relay_up, relay_down]:
        cp.wait_send()


def prepare(block_lists, key_blocks):
    flat = block_lists.reshape(ENT)
    col = jnp.broadcast_to(flat[:, None], (ENT, 128))
    row = jnp.broadcast_to(jnp.pad(flat, (0, 128 - ENT))[None], (8, 128))
    lists = jnp.concatenate([col, row], axis=0)
    dma = pltpu.SemaphoreType.DMA
    vmem = pl.BlockSpec(memory_space=pltpu.VMEM)
    any_ = pl.BlockSpec(memory_space=pl.ANY)
    return pl.pallas_call(
        prepare_kernel,
        out_shape=(
            jax.ShapeDtypeStruct((NY * SHARD, ROWS, HD), BF16),
            jax.ShapeDtypeStruct((16, 128), jnp.int32),
            jax.ShapeDtypeStruct((8, 128), jnp.int32),
        ),
        in_specs=[vmem, any_],
        out_specs=(any_, vmem, vmem),
        scratch_shapes=[
            pltpu.VMEM((NZ, ENT + 8, 128), jnp.int32),
            pltpu.VMEM((NY, 8, 128), jnp.int32),
            dma((NZ - 1,)),
            dma((NZ - 1,)),
            dma((NY - 1,)),
            dma((NY - 1,)),
            dma((4,)),
            dma((4,)),
            dma((1,)),
        ],
        compiler_params=pltpu.CompilerParams(collective_id=0, has_side_effects=True),
        name="prepare",
    )(lists, key_blocks)


def main_kernel(
    caps,
    tab,
    first_hbm,
    q_hbm,
    nk_hbm,
    nv_hbm,
    kc_hbm,
    vc_hbm,
    w_hbm,
    out_ref,
    cols,
    hops,
    fins,
    kg,
    vg,
    q,
    probs,
    att,
    w_all,
    w_relay,
    acc,
    v_own,
    v_new,
    y_send,
    y_recv,
    z_send,
    z_recv,
    w_send,
    w_recv,
    a_send,
    a_recv,
    local_sem,
):
    s = lax.axis_index("seq")
    t = lax.axis_index("tp")
    y, z = s // NZ, lax.rem(s, NZ)
    x, c = t // NC, lax.rem(t, NC)
    yp = lax.rem(y + 1, NY) * NZ + z
    ym = lax.rem(y + NY - 1, NY) * NZ + z
    zp = y * NZ + lax.rem(z + 1, NZ)
    zm = y * NZ + lax.rem(z + NZ - 1, NZ)
    xp = lax.rem(x + 1, NX)
    xm = lax.rem(x + NX - 1, NX)
    xo = lax.rem(x + 2, NX)
    sib = x * NC + (1 - c)

    def remote(src, dst, ssem, rsem, seq=None, tp=None):
        return pltpu.make_async_remote_copy(
            src_ref=src,
            dst_ref=dst,
            send_sem=ssem,
            recv_sem=rsem,
            device_id={"seq": s if seq is None else seq, "tp": t if tp is None else tp},
            device_id_type=MESH,
        )

    barrier = pltpu.get_barrier_semaphore()
    peers = [(yp, t), (ym, t), (zp, t), (zm, t), (s, sib)]
    peers += [(s, xx * NC + cc) for xx in (xp, xm) for cc in range(NC)]
    for ps, pt in peers:
        pl.semaphore_signal(
            barrier, inc=1, device_id={"seq": ps, "tp": pt}, device_id_type=MESH
        )

    pending = []

    locals_ = []

    def local(src, dst):
        cp = pltpu.make_async_copy(src, dst, local_sem.at[len(locals_)])
        cp.start()
        locals_.append(cp)
        return cp

    def source(ch):
        if ch < PARTS:
            return kc_hbm.at[:, pl.ds(ch * ROWS, ROWS), :]
        return cols[ch].at[own_rows]

    own_rows = pl.ds(pl.multiple_of(y * SHARD, SHARD), SHARD)
    own_cols = [local(first_hbm, cols[0])]
    own_cols += [local(source(ch), cols[ch].at[own_rows]) for ch in range(1, PARTS)]
    in_v = local(vc_hbm, v_own)
    in_q = local(q_hbm, q)
    in_nk = [local(nk_hbm.at[pl.ds(b * BLOCK, BLOCK)], kg.at[b, pl.ds(TOPB * BLOCK, BLOCK)]) for b in range(QBD)]
    in_nv = local(nv_hbm, v_new)

    pl.semaphore_wait(barrier, len(peers))

    half = SHARD // 2
    y_copies = {}

    def y_start(ch):
        mine = [
            remote(source(ch), cols[ch].at[own_rows], y_send.at[ch, 0], y_recv.at[ch, 0], seq=yp),
            remote(source(ch), cols[ch].at[own_rows], y_send.at[ch, 1], y_recv.at[ch, 1], seq=ym),
        ]
        for cp in mine:
            cp.start()
        y_copies[ch] = mine
        pending.extend(mine)

    def y_relay(ch):
        first, second = y_copies[ch]
        first.wait_recv()
        lo = pl.ds(pl.multiple_of(lax.rem(y + NY - 1, NY) * SHARD, SHARD), half)
        a = remote(cols[ch].at[lo], cols[ch].at[lo], y_send.at[ch, 2], y_recv.at[ch, 2], seq=yp)
        a.start()
        second.wait_recv()
        hi = pl.ds(pl.multiple_of(lax.rem(y + 1, NY) * SHARD + half, half), half)
        b = remote(cols[ch].at[hi], cols[ch].at[hi], y_send.at[ch, 3], y_recv.at[ch, 3], seq=ym)
        b.start()
        pending.extend([a, b])
        return a, b

    z_copies = {}
    seg = 2

    def merge(ch, d, step):
        cap = caps[step]
        kept = caps[step - 1] if step else 0
        buf = hops[d][step][ch]

        def fresh(j):
            at = tab[d * 4 + step, j]
            return at, cols[ch][jnp.maximum(at, 0)]

        def both(i, carry):
            for u in range(seg):
                j = i * seg + u
                at, new = fresh(j)
                buf[j] = jnp.where(at < 0, buf[j], new)
            return carry

        def only(i, carry):
            for u in range(seg):
                j = i * seg + u
                buf[j] = fresh(j)[1]
            return carry

        if kept:
            lax.fori_loop(0, kept // seg, both, 0)
        if cap > kept:
            lax.fori_loop(kept // seg, cap // seg, only, 0)

    def z_step(ch, step):
        if ch == 0 and step == 0:
            own_cols[0].wait()
        for d in range(2):
            if step:
                z_copies[ch, d, step - 1].wait_recv()
            merge(ch, d, step)
            if step < 3:
                dst = hops[d][step + 1][ch].at[pl.ds(0, caps[step])]
            else:
                dst = fins[d][ch]
            cp = remote(
                hops[d][step][ch],
                dst,
                z_send.at[ch, d, step],
                z_recv.at[ch, d, step],
                seq=zp if d == 0 else zm,
            )
            cp.start()
            z_copies[ch, d, step] = cp
            pending.append(cp)

    def collect(ch):
        for d in range(2):
            z_copies[ch, d, 3].wait_recv()
        r0 = (ch % PARTS) * ROWS
        for b in range(QBD):

            def entry(i, carry):
                e = b * TOPB + i
                way = tab[8, e]
                val = jnp.where(
                    way == 0,
                    cols[ch][tab[11, e]],
                    jnp.where(way == 1, fins[0][ch][tab[9, e]], fins[1][ch][tab[10, e]]),
                )
                at = pl.multiple_of(i * BLOCK, BLOCK)
                if ch < PARTS:
                    kg[b, pl.ds(at + r0, ROWS), :] = val
                else:
                    vg[b, pl.ds(r0, ROWS), pl.ds(at, BLOCK)] = val
                return carry

            lax.fori_loop(0, TOPB, entry, 0)

    def turn(i):
        if i == 0:
            in_v.wait()
            in_nv.wait()
        n = SHARD // QBD

        def block(j, carry):
            blk = i * n + j
            flipped = v_own[blk].T
            for p in range(PARTS):
                cols[PARTS + p][y * SHARD + blk] = flipped[p * ROWS : (p + 1) * ROWS]
            return carry

        lax.fori_loop(0, n, block, 0)
        vg[i, :, TOPB * BLOCK :] = v_new[i * BLOCK : (i + 1) * BLOCK, :].T

    width = w_hbm.shape[3] // TP
    hg = G // 2

    def w_cols(tt):
        return pl.ds(pl.multiple_of(tt * width, width), width)

    w_direct, w_first = [], []

    def w_start():
        targets = [sib] + [xx * NC + cc for xx in (xp, xm) for cc in range(NC)]
        slots = [0, 1 + c, 1 + c, 3 + c, 3 + c]
        for dirn in range(2):
            for cc in range(NC):
                cp = remote(
                    w_hbm.at[pl.ds(dirn * hg, hg), :, :, w_cols(xo * NC + cc)],
                    w_relay.at[dirn * NC + cc],
                    w_send.at[5 + dirn * NC + cc],
                    w_recv.at[5 + dirn * NC + cc],
                    tp=(xp if dirn == 0 else xm) * NC + c,
                )
                cp.start()
                w_first.append(cp)
                pending.append(cp)
        for i, (tt, slot) in enumerate(zip(targets, slots)):
            cp = remote(
                w_hbm.at[:, :, :, w_cols(tt)],
                w_all.at[t],
                w_send.at[i],
                w_recv.at[slot],
                tp=tt,
            )
            cp.start()
            w_direct.append(cp)
            pending.append(cp)

    w_second = []

    def w_forward():
        for dirn in range(2):
            for cc in range(NC):
                w_first[dirn * NC + cc].wait_recv()
                src_t = (xm if dirn == 0 else xp) * NC + c
                dst_t = (xp if dirn == 0 else xm) * NC + cc
                cp = remote(
                    w_relay.at[dirn * NC + cc],
                    w_all.at[src_t, pl.ds(dirn * hg, hg)],
                    w_send.at[9 + dirn * NC + cc],
                    w_recv.at[9 + dirn * NC + c],
                    tp=dst_t,
                )
                cp.start()
                w_second.append(cp)
                pending.append(cp)

    def w_wait():
        for slot in range(5):
            remote(
                w_hbm.at[:, :, :, w_cols(t)], w_all.at[t], w_send.at[0], w_recv.at[slot], tp=sib
            ).wait_recv()
        for slot in range(4):
            remote(
                w_relay.at[slot],
                w_all.at[t, pl.ds(0, hg)],
                w_send.at[9],
                w_recv.at[9 + slot],
                tp=sib,
            ).wait_recv()

    y_start(1)
    w_own = local(w_hbm.at[:, :, :, w_cols(t)], w_all.at[t])
    w_start()

    relays = {}

    def y_first(ch):
        if ch < PARTS:
            own_cols[ch].wait()
        relays[ch] = y_relay(ch)
        if ch + 1 < CHUNKS:
            y_start(ch + 1)

    def y_second(ch):
        for cp in relays[ch]:
            cp.wait_recv()

    def scores(b):
        rows = pl.ds(pl.multiple_of(b * BLOCK, BLOCK), BLOCK)
        keys = kg[b]
        seen = TOPB * BLOCK
        row_ids = lax.broadcasted_iota(jnp.int32, (BLOCK, BLOCK), 0)
        col_ids = lax.broadcasted_iota(jnp.int32, (BLOCK, BLOCK), 1)

        def head(g, carry):
            lanes = pl.ds(pl.multiple_of(g * HD, HD), HD)
            out = pl.ds(pl.multiple_of(g * BLOCK, BLOCK), BLOCK)
            sc = lax.dot_general(
                q[rows, lanes], keys, (((1,), (1,)), ((), ())), preferred_element_type=F32
            ) * (1.0 / math.sqrt(HD))
            near = jnp.where(col_ids <= row_ids, sc[:, seen:], -1e30)
            far = sc[:, :seen]
            top = jnp.maximum(
                jnp.max(far, axis=1, keepdims=True), jnp.max(near, axis=1, keepdims=True)
            )
            ef = jnp.exp(far - top)
            en = jnp.exp(near - top)
            tot = jnp.sum(ef, axis=1, keepdims=True) + jnp.sum(en, axis=1, keepdims=True)
            inv = 1.0 / tot
            probs[b, out, :seen] = (ef * inv).astype(BF16)
            probs[b, out, seen:] = (en * inv).astype(BF16)
            return carry

        lax.fori_loop(0, G, head, 0)

    half_d = HD // 2

    def mix(h, b):
        values = vg[b, h * half_d : (h + 1) * half_d, :]
        for g in range(G):
            o = lax.dot_general(
                probs[b, g * BLOCK : (g + 1) * BLOCK, :],
                values,
                (((1,), (1,)), ((), ())),
                preferred_element_type=F32,
            )
            att[t, h, b, :, g * half_d : (g + 1) * half_d] = o.astype(BF16)

    hb = BLOCK // 2
    a_first, a_second, a_third = {}, {}, {}

    def sem(k, i):
        return a_send.at[k[0] * QBD + k[1], i], a_recv.at[k[0] * QBD + k[1], i]

    def stage_a(*k):
        mix(*k)
        own = att.at[t, k[0], k[1]]
        cps = [
            remote(own, own, *sem(k, i), tp=tt)
            for i, tt in enumerate((xp * NC + c, xm * NC + c, sib))
        ]
        for cp in cps:
            cp.start()
        a_first[k] = cps
        pending.extend(cps)

    lo, hi = pl.ds(0, hb), pl.ds(hb, hb)

    def stage_b(*k):
        tm, tpl = xm * NC + c, xp * NC + c
        got = att.at[tm, k[0], k[1]]
        a_first[k][0].wait_recv()
        cps = [
            remote(got.at[lo], got.at[lo], *sem(k, 3), tp=tpl),
            remote(got, got, *sem(k, 4), tp=sib),
        ]
        for cp in cps:
            cp.start()
        got = att.at[tpl, k[0], k[1]]
        a_first[k][1].wait_recv()
        more = [
            remote(got.at[hi], got.at[hi], *sem(k, 5), tp=tm),
            remote(got, got, *sem(k, 6), tp=sib),
        ]
        for cp in more:
            cp.start()
        a_second[k] = cps + more
        pending.extend(a_second[k])

    def stage_c(*k):
        got = att.at[xo * NC + c, k[0], k[1]]
        a_second[k][0].wait_recv()
        a_second[k][2].wait_recv()
        cp = remote(got, got, *sem(k, 7), tp=sib)
        cp.start()
        a_third[k] = cp
        pending.append(cp)

    w_ready = []

    def stage_d(*k):
        h, b = k
        if not w_ready:
            w_ready.append(True)
            w_own.wait()
            w_wait()
        a_first[k][2].wait_recv()
        a_second[k][1].wait_recv()
        a_second[k][3].wait_recv()
        a_third[k].wait_recv()
        rows = slice(b * BLOCK, (b + 1) * BLOCK)
        if not h:
            acc[rows, :] = jnp.zeros((BLOCK, width), F32)

            def term(tt, carry):
                weights = w_all[tt, :, h].reshape(G * half_d, width)
                acc[rows, :] += jnp.dot(att[tt, h, b], weights, preferred_element_type=F32)
                return carry

            lax.fori_loop(0, TP, term, 0)
        else:
            part = acc[rows, :]
            for tt in range(TP):
                part += jnp.dot(
                    att[tt, h, b],
                    w_all[tt, :, h].reshape(G * half_d, width),
                    preferred_element_type=F32,
                )
            out_ref[rows, :] = part.astype(BF16)

    seen_scores = 0
    for step in ORDER:
        kind, ch = step[:2]
        if kind == "ya":
            y_first(ch)
        elif kind == "yb":
            y_second(ch)
            if ch == 3:
                w_forward()
        elif kind == "z":
            z_step(ch, step[2])
        elif kind == "f":
            collect(ch)
        elif kind == "v":
            turn(ch)
        elif kind == "s":
            if not seen_scores:
                in_q.wait()
                for cp in in_nk:
                    cp.wait()
            seen_scores += 1
            scores(ch)
        else:
            {"A": stage_a, "B": stage_b, "C": stage_c, "D": stage_d}[kind](ch, step[2])

    for cp in pending:
        cp.wait_send()


def exchange(level, table, first, queries, new_keys, new_values, key_cache, value_cache, out_weight):
    caps = LEVELS[level]
    any_ = pl.BlockSpec(memory_space=pl.ANY)
    width = out_weight.shape[3] // TP
    blk = lambda n: pltpu.VMEM((n, ROWS, HD), BF16)
    hop_bufs = [[[blk(caps[i]) for _ in range(CHUNKS)] for i in range(4)] for _ in range(2)]
    fin_bufs = [[blk(caps[3]) for _ in range(CHUNKS)] for _ in range(2)]
    scratch = [
        [blk(NY * SHARD) for _ in range(CHUNKS)],
        hop_bufs,
        fin_bufs,
        pltpu.VMEM((QBD, (TOPB + 1) * BLOCK, HD), BF16),
        pltpu.VMEM((QBD, HD, (TOPB + 1) * BLOCK), BF16),
        pltpu.VMEM((QBD * BLOCK, G * HD), BF16),
        pltpu.VMEM((QBD, G * BLOCK, (TOPB + 1) * BLOCK), BF16),
        pltpu.VMEM((TP, 2, QBD, BLOCK, G * HD // 2), BF16),
        pltpu.VMEM((TP, G, 2, HD // 2, width), BF16),
        pltpu.VMEM((4, G // 2, 2, HD // 2, width), BF16),
        pltpu.VMEM((QBD * BLOCK, width), F32),
        pltpu.VMEM((SHARD, BLOCK, HD), BF16),
        pltpu.VMEM((QBD * BLOCK, HD), BF16),
        pltpu.SemaphoreType.DMA((CHUNKS, 4)),
        pltpu.SemaphoreType.DMA((CHUNKS, 4)),
        pltpu.SemaphoreType.DMA((CHUNKS, 2, 4)),
        pltpu.SemaphoreType.DMA((CHUNKS, 2, 4)),
        pltpu.SemaphoreType.DMA((13,)),
        pltpu.SemaphoreType.DMA((13,)),
        pltpu.SemaphoreType.DMA((2 * QBD, 8)),
        pltpu.SemaphoreType.DMA((2 * QBD, 8)),
        pltpu.SemaphoreType.DMA((PARTS + 4 + QBD,)),
    ]
    flat, tree = jax.tree.flatten(scratch)
    fixed = 9

    def kernel(*refs):
        main_kernel(caps, *refs[:fixed], *jax.tree.unflatten(tree, refs[fixed:]))

    return pl.pallas_call(
        kernel,
        out_shape=jax.ShapeDtypeStruct((QBD * BLOCK, width), BF16),
        in_specs=[pl.BlockSpec(memory_space=pltpu.SMEM)] + [any_] * 7,
        out_specs=pl.BlockSpec(memory_space=pltpu.VMEM),
        scratch_shapes=flat,
        compiler_params=pltpu.CompilerParams(
            collective_id=1 + level, has_side_effects=True, vmem_limit_bytes=60 * 1024 * 1024
        ),
        name="exchange",
    )(
        table,
        first,
        queries,
        new_keys,
        new_values,
        key_cache,
        value_cache,
        out_weight,
    )


def body(queries, new_keys, new_values, key_cache, value_cache, block_lists, out_weight):
    key_blocks = key_cache.reshape(SHARD, BLOCK, HD)
    value_blocks = value_cache.reshape(SHARD, BLOCK, HD)
    first, table, level = prepare(block_lists, key_blocks)
    branches = [functools.partial(exchange, i) for i in range(len(LEVELS))]
    return lax.switch(
        level[0, 0],
        branches,
        table,
        first,
        queries,
        new_keys,
        new_values,
        key_blocks,
        value_blocks,
        out_weight.reshape(G, 2, HD // 2, -1),
    )


def solution(mesh):
    in_specs = (
        P("seq", "tp"),
        P("seq", "tp"),
        P("seq", "tp"),
        P("seq", "tp"),
        P("seq", "tp"),
        P("seq", None),
        P("tp", None),
    )
    out_specs = P("seq", "tp")
    return jax.shard_map(body, mesh=mesh, in_specs=in_specs, out_specs=out_specs, check_vma=False)
```

```python
import functools
import math

import jax
import jax.numpy as jnp
from jax import lax
from jax.experimental import pallas as pl
from jax.experimental.pallas import tpu as pltpu
from jax.sharding import PartitionSpec as P

HD = 128
BLOCK = 128
TOPB = 8
NY, NZ, NX, NC = 4, 8, 4, 2
SEQ = NY * NZ
TP = NX * NC
SHARD = 32
QBD = 4
ENT = QBD * TOPB
G = 4
LEVELS = ((8, 14, 18, 22), (8, 16, 22, 26), (8, 24, 32, 32))
SPLIT = 8
PARTS = 4
ROWS = BLOCK // PARTS
CHUNKS = 2 * PARTS
MESH = pl.DeviceIdType.MESH
F32 = jnp.float32
BF16 = jnp.bfloat16


ORDER = (
    ("z", 0, 0),
    ("v", 0),
    ("z", 0, 1),
    ("v", 1),
    ("v", 2),
    ("ya", 1),
    ("yb", 1),
    ("z", 1, 0),
    ("z", 0, 2),
    ("ya", 2),
    ("v", 3),
    ("z", 0, 3),
    ("yb", 2),
    ("z", 2, 0),
    ("z", 1, 1),
    ("z", 2, 1),
    ("ya", 3),
    ("f", 0),
    ("z", 1, 2),
    ("yb", 3),
    ("z", 3, 0),
    ("z", 2, 2),
    ("z", 3, 1),
    ("ya", 4),
    ("z", 2, 3),
    ("yb", 4),
    ("z", 1, 3),
    ("z", 4, 0),
    ("f", 2),
    ("z", 3, 2),
    ("ya", 5),
    ("z", 4, 1),
    ("f", 1),
    ("yb", 5),
    ("z", 5, 0),
    ("z", 3, 3),
    ("z", 5, 1),
    ("ya", 6),
    ("z", 4, 2),
    ("f", 3),
    ("s", 0),
    ("yb", 6),
    ("z", 6, 0),
    ("z", 5, 2),
    ("z", 6, 1),
    ("ya", 7),
    ("z", 4, 3),
    ("s", 1),
    ("yb", 7),
    ("z", 7, 0),
    ("z", 5, 3),
    ("z", 7, 1),
    ("s", 2),
    ("z", 6, 2),
    ("f", 4),
    ("s", 3),
    ("f", 5),
    ("z", 7, 2),
    ("A", 0, 0),
    ("z", 6, 3),
    ("A", 0, 1),
    ("A", 0, 2),
    ("z", 7, 3),
    ("B", 0, 0),
    ("A", 0, 3),
    ("B", 0, 1),
    ("f", 6),
    ("B", 0, 3),
    ("C", 0, 0),
    ("C", 0, 1),
    ("B", 0, 2),
    ("f", 7),
    ("A", 1, 0),
    ("A", 1, 1),
    ("A", 1, 2),
    ("A", 1, 3),
    ("D", 0, 1),
    ("B", 1, 0),
    ("C", 0, 2),
    ("B", 1, 1),
    ("D", 0, 0),
    ("B", 1, 2),
    ("C", 0, 3),
    ("B", 1, 3),
    ("C", 1, 0),
    ("C", 1, 1),
    ("D", 0, 2),
    ("C", 1, 2),
    ("D", 0, 3),
    ("C", 1, 3),
    ("D", 1, 0),
    ("D", 1, 1),
    ("D", 1, 2),
    ("D", 1, 3),
)


def total(mask, axis):
    return jnp.sum(jnp.where(mask, 1, 0), axis=axis, keepdims=True)


def prepare_kernel(
    lists, kc_hbm, cols_out, tab_out, level_out, every, levels, l_send, l_recv, v_send, v_recv, y_send, y_recv, sem
):
    s = lax.axis_index("seq")
    y, z = s // NZ, lax.rem(s, NZ)
    yp = lax.rem(y + 1, NY)
    ym = lax.rem(y + NY - 1, NY)

    barrier = pltpu.get_barrier_semaphore()
    ring_z = [y * NZ + lax.rem(z + i, NZ) for i in range(1, NZ)]
    ring_y = [lax.rem(y + i, NY) * NZ + z for i in range(1, NY)]
    for peer in ring_z + ring_y:
        pl.semaphore_signal(barrier, inc=1, device_id={"seq": peer}, device_id_type=MESH)

    own_rows = pl.ds(pl.multiple_of(y * SHARD, SHARD), SHARD)
    mine = kc_hbm.at[:, pl.ds(0, ROWS), :]
    keep = pltpu.make_async_copy(mine, cols_out.at[own_rows], sem.at[0])
    keep.start()
    every[z] = lists[...]
    pl.semaphore_wait(barrier, NZ + NY - 2)

    def remote(src, dst, ssem, rsem, seq):
        return pltpu.make_async_remote_copy(
            src_ref=src,
            dst_ref=dst,
            send_sem=ssem,
            recv_sem=rsem,
            device_id={"seq": seq},
            device_id_type=MESH,
        )

    told = [
        remote(lists, every.at[z], l_send.at[i], l_recv.at[i], peer) for i, peer in enumerate(ring_z)
    ]
    for cp in told:
        cp.start()
    half = SHARD // 2
    direct = []
    for turn in range(2):
        for i, seq in enumerate((yp, ym)):
            part = (i + turn) % 2
            rows = pl.ds(pl.multiple_of(y * SHARD + part * half, half), half)
            cp = remote(
                kc_hbm.at[pl.ds(part * half, half), pl.ds(0, ROWS), :],
                cols_out.at[rows],
                y_send.at[2 * turn + i],
                y_recv.at[2 * turn + i],
                seq * NZ + z,
            )
            cp.start()
            direct.append(cp)
    lo = pl.ds(pl.multiple_of(ym * SHARD, half), half)
    hi = pl.ds(pl.multiple_of(yp * SHARD + half, half), half)
    direct[0].wait_recv()
    relay_up = remote(cols_out.at[lo], cols_out.at[lo], y_send.at[4], y_recv.at[4], yp * NZ + z)
    relay_up.start()
    direct[1].wait_recv()
    relay_down = remote(cols_out.at[hi], cols_out.at[hi], y_send.at[5], y_recv.at[5], ym * NZ + z)
    relay_down.start()
    for cp in told:
        cp.wait_recv()

    shape = (ENT, 128)
    e_col = lax.broadcasted_iota(jnp.int32, shape, 0)
    e_row = lax.broadcasted_iota(jnp.int32, shape, 1)
    valid = e_row < ENT
    need = jnp.zeros((1, 1), jnp.int32)
    for k in range(NZ):
        zk = lax.rem(z + k, NZ)
        col = every[zk, :ENT]
        row = jnp.broadcast_to(every[zk, ENT : ENT + 1], shape)
        spot_col = (col >> 8) * SHARD + (col & (SHARD - 1))
        du_col = (zk - ((col >> 5) & (NZ - 1))) & (NZ - 1)
        du_row = (zk - ((row >> 5) & (NZ - 1))) & (NZ - 1)
        n_up = total((du_row >= 1) & (du_row <= 3) & valid, 1)[:1]
        n_down = total((du_row >= 5) & valid, 1)[:1]
        n_half = total((du_row == 4) & valid, 1)[:1]
        share = (n_half + n_down - n_up + 1) >> 1
        share = jnp.minimum(jnp.maximum(share, n_half - SPLIT), jnp.minimum(n_half, SPLIT))
        share = jnp.maximum(share, 0)
        rank_col = total((e_row < e_col) & (du_row == 4) & valid, 1)
        rank_row = total((e_col < e_row) & (du_col == 4), 0)

        def routed(du, rank, bad):
            first = rank < share
            up = ((du >= 1) & (du <= 3)) | ((du == 4) & first)
            down = (du >= 5) | ((du == 4) & jnp.logical_not(first))
            way = jnp.where(up, 1, jnp.where(down, 2, 0))
            way = jnp.where(bad, 3, way)
            dist = jnp.where(down, NZ - du, du)
            return way, dist

        way_col, dist_col = routed(du_col, rank_col, e_row < 0)
        way_row, dist_row = routed(du_row, rank_row, jnp.logical_not(valid))
        order_col = (NZ - dist_col) * ENT + e_col
        order_row = (NZ - dist_row) * ENT + e_row
        same = way_col == way_row
        place_col = total(same & (order_row < order_col), 1)

        for i in range(4):
            for way in (1, 2):
                count = total((way_row == way) & (dist_row >= 4 - i), 1)[:1]
                for level in range(len(LEVELS) - 1):
                    over = jnp.where(count > LEVELS[level][i], level + 1, 0)
                    need = jnp.maximum(need, over)

        def pick(way, dist):
            hit = (way_col == way) & (dist_col == dist) & (place_col == e_row)
            return jnp.sum(jnp.where(hit, spot_col + 1, 0), axis=0, keepdims=True) - 1

        if 1 <= k <= 4:
            tab_out[4 - k : 5 - k, :] = pick(1, k)
        if k >= 4:
            tab_out[k : k + 1, :] = pick(2, NZ - k)
        if k == 0:
            place_row = total(same & (order_col < order_row), 0)
            way = way_row[:1]
            spot = ((row >> 8) * SHARD + (row & (SHARD - 1)))[:1]
            tab_out[8:9, :] = way
            tab_out[9:10, :] = jnp.where(way == 1, place_row, 0)
            tab_out[10:11, :] = jnp.where(way == 2, place_row, 0)
            tab_out[11:12, :] = jnp.where(way == 0, spot, 0)
            tab_out[12:16, :] = jnp.zeros((4, 128), jnp.int32)

    levels[y] = jnp.broadcast_to(need, (8, 128))
    agree = [
        remote(levels.at[y], levels.at[y], v_send.at[i], v_recv.at[i], peer)
        for i, peer in enumerate(ring_y)
    ]
    for cp in agree:
        cp.start()

    for cp in agree:
        cp.wait_recv()
    level_out[...] = jnp.maximum(
        jnp.maximum(levels[0], levels[1]), jnp.maximum(levels[2], levels[3])
    )
    for cp in (direct[2], direct[3], relay_up, relay_down):
        cp.wait_recv()
    keep.wait()
    for cp in told + direct + agree + [relay_up, relay_down]:
        cp.wait_send()


def prepare(block_lists, key_blocks):
    flat = block_lists.reshape(ENT)
    col = jnp.broadcast_to(flat[:, None], (ENT, 128))
    row = jnp.broadcast_to(jnp.pad(flat, (0, 128 - ENT))[None], (8, 128))
    lists = jnp.concatenate([col, row], axis=0)
    dma = pltpu.SemaphoreType.DMA
    vmem = pl.BlockSpec(memory_space=pltpu.VMEM)
    any_ = pl.BlockSpec(memory_space=pl.ANY)
    return pl.pallas_call(
        prepare_kernel,
        out_shape=(
            jax.ShapeDtypeStruct((NY * SHARD, ROWS, HD), BF16),
            jax.ShapeDtypeStruct((16, 128), jnp.int32),
            jax.ShapeDtypeStruct((8, 128), jnp.int32),
        ),
        in_specs=[vmem, any_],
        out_specs=(any_, vmem, vmem),
        scratch_shapes=[
            pltpu.VMEM((NZ, ENT + 8, 128), jnp.int32),
            pltpu.VMEM((NY, 8, 128), jnp.int32),
            dma((NZ - 1,)),
            dma((NZ - 1,)),
            dma((NY - 1,)),
            dma((NY - 1,)),
            dma((6,)),
            dma((6,)),
            dma((1,)),
        ],
        compiler_params=pltpu.CompilerParams(collective_id=0, has_side_effects=True),
        name="prepare",
    )(lists, key_blocks)


def main_kernel(
    caps,
    tab,
    first_hbm,
    q_hbm,
    nk_hbm,
    nv_hbm,
    kc_hbm,
    vc_hbm,
    w_hbm,
    out_ref,
    cols,
    hops,
    fins,
    kg,
    vg,
    q,
    probs,
    att,
    w_all,
    w_relay,
    acc,
    v_own,
    v_new,
    y_send,
    y_recv,
    z_send,
    z_recv,
    w_send,
    w_recv,
    a_send,
    a_recv,
    local_sem,
):
    s = lax.axis_index("seq")
    t = lax.axis_index("tp")
    y, z = s // NZ, lax.rem(s, NZ)
    x, c = t // NC, lax.rem(t, NC)
    yp = lax.rem(y + 1, NY) * NZ + z
    ym = lax.rem(y + NY - 1, NY) * NZ + z
    zp = y * NZ + lax.rem(z + 1, NZ)
    zm = y * NZ + lax.rem(z + NZ - 1, NZ)
    xp = lax.rem(x + 1, NX)
    xm = lax.rem(x + NX - 1, NX)
    xo = lax.rem(x + 2, NX)
    sib = x * NC + (1 - c)

    def remote(src, dst, ssem, rsem, seq=None, tp=None):
        return pltpu.make_async_remote_copy(
            src_ref=src,
            dst_ref=dst,
            send_sem=ssem,
            recv_sem=rsem,
            device_id={"seq": s if seq is None else seq, "tp": t if tp is None else tp},
            device_id_type=MESH,
        )

    barrier = pltpu.get_barrier_semaphore()
    peers = [(yp, t), (ym, t), (zp, t), (zm, t), (s, sib)]
    peers += [(s, xx * NC + cc) for xx in (xp, xm) for cc in range(NC)]
    for ps, pt in peers:
        pl.semaphore_signal(
            barrier, inc=1, device_id={"seq": ps, "tp": pt}, device_id_type=MESH
        )

    pending = []

    locals_ = []

    def local(src, dst):
        cp = pltpu.make_async_copy(src, dst, local_sem.at[len(locals_)])
        cp.start()
        locals_.append(cp)
        return cp

    def source(ch):
        if ch < PARTS:
            return kc_hbm.at[:, pl.ds(ch * ROWS, ROWS), :]
        return cols[ch].at[own_rows]

    own_rows = pl.ds(pl.multiple_of(y * SHARD, SHARD), SHARD)
    own_cols = [local(first_hbm, cols[0])]
    own_cols += [local(source(ch), cols[ch].at[own_rows]) for ch in range(1, PARTS)]
    in_v = local(vc_hbm, v_own)
    in_q = local(q_hbm, q)
    in_nk = [local(nk_hbm.at[pl.ds(b * BLOCK, BLOCK)], kg.at[b, pl.ds(TOPB * BLOCK, BLOCK)]) for b in range(QBD)]
    in_nv = local(nv_hbm, v_new)

    pl.semaphore_wait(barrier, len(peers))

    half = SHARD // 2
    y_copies = {}

    def y_start(ch):
        mine = [
            remote(source(ch), cols[ch].at[own_rows], y_send.at[ch, 0], y_recv.at[ch, 0], seq=yp),
            remote(source(ch), cols[ch].at[own_rows], y_send.at[ch, 1], y_recv.at[ch, 1], seq=ym),
        ]
        for cp in mine:
            cp.start()
        y_copies[ch] = mine
        pending.extend(mine)

    def y_relay(ch):
        first, second = y_copies[ch]
        first.wait_recv()
        lo = pl.ds(pl.multiple_of(lax.rem(y + NY - 1, NY) * SHARD, SHARD), half)
        a = remote(cols[ch].at[lo], cols[ch].at[lo], y_send.at[ch, 2], y_recv.at[ch, 2], seq=yp)
        a.start()
        second.wait_recv()
        hi = pl.ds(pl.multiple_of(lax.rem(y + 1, NY) * SHARD + half, half), half)
        b = remote(cols[ch].at[hi], cols[ch].at[hi], y_send.at[ch, 3], y_recv.at[ch, 3], seq=ym)
        b.start()
        pending.extend([a, b])
        return a, b

    z_copies = {}
    seg = 2

    def merge(ch, d, step):
        cap = caps[step]
        kept = caps[step - 1] if step else 0
        buf = hops[d][step][ch]

        def fresh(j):
            at = tab[d * 4 + step, j]
            return at, cols[ch][jnp.maximum(at, 0)]

        def both(i, carry):
            for u in range(seg):
                j = i * seg + u
                at, new = fresh(j)
                buf[j] = jnp.where(at < 0, buf[j], new)
            return carry

        def only(i, carry):
            for u in range(seg):
                j = i * seg + u
                buf[j] = fresh(j)[1]
            return carry

        if kept:
            lax.fori_loop(0, kept // seg, both, 0)
        if cap > kept:
            lax.fori_loop(kept // seg, cap // seg, only, 0)

    def z_step(ch, step):
        if ch == 0 and step == 0:
            own_cols[0].wait()
        for d in range(2):
            if step:
                z_copies[ch, d, step - 1].wait_recv()
            merge(ch, d, step)
            if step < 3:
                dst = hops[d][step + 1][ch].at[pl.ds(0, caps[step])]
            else:
                dst = fins[d][ch]
            cp = remote(
                hops[d][step][ch],
                dst,
                z_send.at[ch, d, step],
                z_recv.at[ch, d, step],
                seq=zp if d == 0 else zm,
            )
            cp.start()
            z_copies[ch, d, step] = cp
            pending.append(cp)

    def collect(ch):
        for d in range(2):
            z_copies[ch, d, 3].wait_recv()
        r0 = (ch % PARTS) * ROWS
        for b in range(QBD):

            def entry(i, carry):
                e = b * TOPB + i
                way = tab[8, e]
                val = jnp.where(
                    way == 0,
                    cols[ch][tab[11, e]],
                    jnp.where(way == 1, fins[0][ch][tab[9, e]], fins[1][ch][tab[10, e]]),
                )
                at = pl.multiple_of(i * BLOCK, BLOCK)
                if ch < PARTS:
                    kg[b, pl.ds(at + r0, ROWS), :] = val
                else:
                    vg[b, pl.ds(r0, ROWS), pl.ds(at, BLOCK)] = val
                return carry

            lax.fori_loop(0, TOPB, entry, 0)

    def turn(i):
        if i == 0:
            in_v.wait()
            in_nv.wait()
        n = SHARD // QBD

        def block(j, carry):
            blk = i * n + j
            flipped = v_own[blk].T
            for p in range(PARTS):
                cols[PARTS + p][y * SHARD + blk] = flipped[p * ROWS : (p + 1) * ROWS]
            return carry

        lax.fori_loop(0, n, block, 0)
        vg[i, :, TOPB * BLOCK :] = v_new[i * BLOCK : (i + 1) * BLOCK, :].T

    width = w_hbm.shape[3] // TP
    hg = G // 2

    def w_cols(tt):
        return pl.ds(pl.multiple_of(tt * width, width), width)

    w_direct, w_first = [], []

    def w_start():
        targets = [sib] + [xx * NC + cc for xx in (xp, xm) for cc in range(NC)]
        slots = [0, 1 + c, 1 + c, 3 + c, 3 + c]
        for dirn in range(2):
            for cc in range(NC):
                cp = remote(
                    w_hbm.at[pl.ds(dirn * hg, hg), :, :, w_cols(xo * NC + cc)],
                    w_relay.at[dirn * NC + cc],
                    w_send.at[5 + dirn * NC + cc],
                    w_recv.at[5 + dirn * NC + cc],
                    tp=(xp if dirn == 0 else xm) * NC + c,
                )
                cp.start()
                w_first.append(cp)
                pending.append(cp)
        for i, (tt, slot) in enumerate(zip(targets, slots)):
            cp = remote(
                w_hbm.at[:, :, :, w_cols(tt)],
                w_all.at[t],
                w_send.at[i],
                w_recv.at[slot],
                tp=tt,
            )
            cp.start()
            w_direct.append(cp)
            pending.append(cp)

    w_second = []

    def w_forward():
        for dirn in range(2):
            for cc in range(NC):
                w_first[dirn * NC + cc].wait_recv()
                src_t = (xm if dirn == 0 else xp) * NC + c
                dst_t = (xp if dirn == 0 else xm) * NC + cc
                cp = remote(
                    w_relay.at[dirn * NC + cc],
                    w_all.at[src_t, pl.ds(dirn * hg, hg)],
                    w_send.at[9 + dirn * NC + cc],
                    w_recv.at[9 + dirn * NC + c],
                    tp=dst_t,
                )
                cp.start()
                w_second.append(cp)
                pending.append(cp)

    def w_wait():
        for slot in range(5):
            remote(
                w_hbm.at[:, :, :, w_cols(t)], w_all.at[t], w_send.at[0], w_recv.at[slot], tp=sib
            ).wait_recv()
        for slot in range(4):
            remote(
                w_relay.at[slot],
                w_all.at[t, pl.ds(0, hg)],
                w_send.at[9],
                w_recv.at[9 + slot],
                tp=sib,
            ).wait_recv()

    y_start(1)
    w_own = local(w_hbm.at[:, :, :, w_cols(t)], w_all.at[t])
    w_start()

    relays = {}

    def y_first(ch):
        if ch < PARTS:
            own_cols[ch].wait()
        relays[ch] = y_relay(ch)
        if ch + 1 < CHUNKS:
            y_start(ch + 1)

    def y_second(ch):
        for cp in relays[ch]:
            cp.wait_recv()

    def scores(b):
        rows = pl.ds(pl.multiple_of(b * BLOCK, BLOCK), BLOCK)
        keys = kg[b]
        seen = TOPB * BLOCK
        row_ids = lax.broadcasted_iota(jnp.int32, (BLOCK, BLOCK), 0)
        col_ids = lax.broadcasted_iota(jnp.int32, (BLOCK, BLOCK), 1)

        def head(g, carry):
            lanes = pl.ds(pl.multiple_of(g * HD, HD), HD)
            out = pl.ds(pl.multiple_of(g * BLOCK, BLOCK), BLOCK)
            sc = lax.dot_general(
                q[rows, lanes], keys, (((1,), (1,)), ((), ())), preferred_element_type=F32
            ) * (1.0 / math.sqrt(HD))
            near = jnp.where(col_ids <= row_ids, sc[:, seen:], -1e30)
            far = sc[:, :seen]
            top = jnp.maximum(
                jnp.max(far, axis=1, keepdims=True), jnp.max(near, axis=1, keepdims=True)
            )
            ef = jnp.exp(far - top)
            en = jnp.exp(near - top)
            tot = jnp.sum(ef, axis=1, keepdims=True) + jnp.sum(en, axis=1, keepdims=True)
            inv = 1.0 / tot
            probs[b, out, :seen] = (ef * inv).astype(BF16)
            probs[b, out, seen:] = (en * inv).astype(BF16)
            return carry

        lax.fori_loop(0, G, head, 0)

    half_d = HD // 2

    def mix(h, b):
        values = vg[b, h * half_d : (h + 1) * half_d, :]
        for g in range(G):
            o = lax.dot_general(
                probs[b, g * BLOCK : (g + 1) * BLOCK, :],
                values,
                (((1,), (1,)), ((), ())),
                preferred_element_type=F32,
            )
            att[t, h, b, :, g * half_d : (g + 1) * half_d] = o.astype(BF16)

    hb = BLOCK // 2
    a_first, a_second, a_third = {}, {}, {}

    def sem(k, i):
        return a_send.at[k[0] * QBD + k[1], i], a_recv.at[k[0] * QBD + k[1], i]

    def stage_a(*k):
        mix(*k)
        own = att.at[t, k[0], k[1]]
        cps = [
            remote(own, own, *sem(k, i), tp=tt)
            for i, tt in enumerate((xp * NC + c, xm * NC + c, sib))
        ]
        for cp in cps:
            cp.start()
        a_first[k] = cps
        pending.extend(cps)

    lo, hi = pl.ds(0, hb), pl.ds(hb, hb)

    def stage_b(*k):
        tm, tpl = xm * NC + c, xp * NC + c
        got = att.at[tm, k[0], k[1]]
        a_first[k][0].wait_recv()
        cps = [
            remote(got.at[lo], got.at[lo], *sem(k, 3), tp=tpl),
            remote(got, got, *sem(k, 4), tp=sib),
        ]
        for cp in cps:
            cp.start()
        got = att.at[tpl, k[0], k[1]]
        a_first[k][1].wait_recv()
        more = [
            remote(got.at[hi], got.at[hi], *sem(k, 5), tp=tm),
            remote(got, got, *sem(k, 6), tp=sib),
        ]
        for cp in more:
            cp.start()
        a_second[k] = cps + more
        pending.extend(a_second[k])

    def stage_c(*k):
        got = att.at[xo * NC + c, k[0], k[1]]
        a_second[k][0].wait_recv()
        a_second[k][2].wait_recv()
        cp = remote(got, got, *sem(k, 7), tp=sib)
        cp.start()
        a_third[k] = cp
        pending.append(cp)

    w_ready = []

    def stage_d(*k):
        h, b = k
        if not w_ready:
            w_ready.append(True)
            w_own.wait()
            w_wait()
        a_first[k][2].wait_recv()
        a_second[k][1].wait_recv()
        a_second[k][3].wait_recv()
        a_third[k].wait_recv()
        rows = slice(b * BLOCK, (b + 1) * BLOCK)
        if not h:
            acc[rows, :] = jnp.zeros((BLOCK, width), F32)

            def term(tt, carry):
                weights = w_all[tt, :, h].reshape(G * half_d, width)
                acc[rows, :] += jnp.dot(att[tt, h, b], weights, preferred_element_type=F32)
                return carry

            lax.fori_loop(0, TP, term, 0)
        else:
            part = acc[rows, :]
            for tt in range(TP):
                part += jnp.dot(
                    att[tt, h, b],
                    w_all[tt, :, h].reshape(G * half_d, width),
                    preferred_element_type=F32,
                )
            out_ref[rows, :] = part.astype(BF16)

    seen_scores = 0
    for step in ORDER:
        kind, ch = step[:2]
        if kind == "ya":
            y_first(ch)
        elif kind == "yb":
            y_second(ch)
            if ch == 3:
                w_forward()
        elif kind == "z":
            z_step(ch, step[2])
        elif kind == "f":
            collect(ch)
        elif kind == "v":
            turn(ch)
        elif kind == "s":
            if not seen_scores:
                in_q.wait()
                for cp in in_nk:
                    cp.wait()
            seen_scores += 1
            scores(ch)
        else:
            {"A": stage_a, "B": stage_b, "C": stage_c, "D": stage_d}[kind](ch, step[2])

    for cp in pending:
        cp.wait_send()


def exchange(level, table, first, queries, new_keys, new_values, key_cache, value_cache, out_weight):
    caps = LEVELS[level]
    any_ = pl.BlockSpec(memory_space=pl.ANY)
    width = out_weight.shape[3] // TP
    blk = lambda n: pltpu.VMEM((n, ROWS, HD), BF16)
    hop_bufs = [[[blk(caps[i]) for _ in range(CHUNKS)] for i in range(4)] for _ in range(2)]
    fin_bufs = [[blk(caps[3]) for _ in range(CHUNKS)] for _ in range(2)]
    scratch = [
        [blk(NY * SHARD) for _ in range(CHUNKS)],
        hop_bufs,
        fin_bufs,
        pltpu.VMEM((QBD, (TOPB + 1) * BLOCK, HD), BF16),
        pltpu.VMEM((QBD, HD, (TOPB + 1) * BLOCK), BF16),
        pltpu.VMEM((QBD * BLOCK, G * HD), BF16),
        pltpu.VMEM((QBD, G * BLOCK, (TOPB + 1) * BLOCK), BF16),
        pltpu.VMEM((TP, 2, QBD, BLOCK, G * HD // 2), BF16),
        pltpu.VMEM((TP, G, 2, HD // 2, width), BF16),
        pltpu.VMEM((4, G // 2, 2, HD // 2, width), BF16),
        pltpu.VMEM((QBD * BLOCK, width), F32),
        pltpu.VMEM((SHARD, BLOCK, HD), BF16),
        pltpu.VMEM((QBD * BLOCK, HD), BF16),
        pltpu.SemaphoreType.DMA((CHUNKS, 4)),
        pltpu.SemaphoreType.DMA((CHUNKS, 4)),
        pltpu.SemaphoreType.DMA((CHUNKS, 2, 4)),
        pltpu.SemaphoreType.DMA((CHUNKS, 2, 4)),
        pltpu.SemaphoreType.DMA((13,)),
        pltpu.SemaphoreType.DMA((13,)),
        pltpu.SemaphoreType.DMA((2 * QBD, 8)),
        pltpu.SemaphoreType.DMA((2 * QBD, 8)),
        pltpu.SemaphoreType.DMA((PARTS + 4 + QBD,)),
    ]
    flat, tree = jax.tree.flatten(scratch)
    fixed = 9

    def kernel(*refs):
        main_kernel(caps, *refs[:fixed], *jax.tree.unflatten(tree, refs[fixed:]))

    return pl.pallas_call(
        kernel,
        out_shape=jax.ShapeDtypeStruct((QBD * BLOCK, width), BF16),
        in_specs=[pl.BlockSpec(memory_space=pltpu.SMEM)] + [any_] * 7,
        out_specs=pl.BlockSpec(memory_space=pltpu.VMEM),
        scratch_shapes=flat,
        compiler_params=pltpu.CompilerParams(
            collective_id=1 + level, has_side_effects=True, vmem_limit_bytes=60 * 1024 * 1024
        ),
        name="exchange",
    )(
        table,
        first,
        queries,
        new_keys,
        new_values,
        key_cache,
        value_cache,
        out_weight,
    )


def body(queries, new_keys, new_values, key_cache, value_cache, block_lists, out_weight):
    key_blocks = key_cache.reshape(SHARD, BLOCK, HD)
    value_blocks = value_cache.reshape(SHARD, BLOCK, HD)
    first, table, level = prepare(block_lists, key_blocks)
    branches = [functools.partial(exchange, i) for i in range(len(LEVELS))]
    return lax.switch(
        level[0, 0],
        branches,
        table,
        first,
        queries,
        new_keys,
        new_values,
        key_blocks,
        value_blocks,
        out_weight.reshape(G, 2, HD // 2, -1),
    )


def solution(mesh):
    in_specs = (
        P("seq", "tp"),
        P("seq", "tp"),
        P("seq", "tp"),
        P("seq", "tp"),
        P("seq", "tp"),
        P("seq", None),
        P("tp", None),
    )
    out_specs = P("seq", "tp")
    return jax.shard_map(body, mesh=mesh, in_specs=in_specs, out_specs=out_specs, check_vma=False)
```
